128 devices in a mesh: group: 16 (over y_hi, x, core), mp: 8 (over z, y_lo).
Axes of the slice: x: 4, y: 4 (y_hi: 2, y_lo: 2; y = y_hi * 2 + y_lo), z: 4, core: 2. Of those that a mesh axis runs over, the one named last changes fastest.
Arguments:
- hidden_in: bfloat16 [8192, 1024], P('group'), may hold values from -8 to 8
- request_ids: int32 [8192], P('group'), may hold values from 63 to 8191, as said below
- w_qkv: float32 [1024, 3072], P(('group', 'mp')), may hold values from -1 to 1
- w_out: float32 [1024, 1024], P(('group', 'mp')), may hold values from -0.1875 to 0.1875
- w_up: float32 [1024, 4096], P(('group', 'mp')), may hold values from -0.1875 to 0.1875
- w_down: float32 [1024, 4096], P(('group', 'mp')), may hold values from -0.09375 to 0.09375
- ln1_gain: float32 [1024], replicated, may hold values from 0.25 to 1.75
- ln1_shift: float32 [1024], replicated, may hold values from -3 to 3
- ln2_gain: float32 [1024], replicated, may hold values from 0.25 to 1.75
- ln2_shift: float32 [1024], replicated, may hold values from -3 to 3
Outputs:
- hidden_out: bfloat16 [8192, 1024], P(('group', 'mp'))
- keys_cache: bfloat16 [8192, 1024], P('group', 'mp')
- values_cache: bfloat16 [8192, 1024], P('group', 'mp')
The draws below stay inside these ranges and needn't reach their ends.
Inputs may be any that keep to these rules, and one draw needn't show every extreme that they name: `request_ids`: each slot holds the index of the last slot of its request. In groups 2i and 2i+1 (of 512 slots each) one request of exactly 512 slots ends the first group and begins the second, at least 64 of its slots in each; every other request lies within one aligned block of 64 slots, one or two requests a block, and some blocks hold one request of exactly 64 slots.
All inputs are finite; a program needn't handle non-finite values.
Results may differ from the reference program's by a relative error of at most 0.011.
Values may be sent and summed in bfloat16 or wider, within the bound.
No kernel may reach another device: no remote copies, remote signals or barrier semaphores. Data moves between devices by JAX's collectives and lax.ppermute only.
A program may use at most 64 MiB of HBM per device.

```python
import jax
import jax.numpy as jnp
from jax import lax

D = 1024
HEADS = 16
HD = 64
FF = 4096
TOK_G = 512
SHORT = 64
TOKENS = 8192
N_GROUP = 16


def draw_hidden_in(key, part):
    base_values = jnp.clip(jax.random.normal(key, (TOKENS, D), jnp.float32), -6.0, 6.0)
    return base_values.astype(jnp.bfloat16)


def draw_w_qkv(key, part):
    base_values = jnp.clip(jax.random.normal(key, (D, 3 * D), jnp.float32), -5.0, 5.0) * D ** (-0.5)
    sharpen = jnp.concatenate([jnp.full((2 * D,), 1.7, jnp.float32), jnp.ones((D,), jnp.float32)])
    base_values = base_values * sharpen
    return jnp.clip(base_values, -1.0, 1.0)


def draw_request_ids(key, part):
    block_total = TOKENS // SHORT
    per_group = TOK_G // SHORT
    pair_total = TOKENS // (2 * TOK_G)
    long_tail = jax.random.randint(jax.random.fold_in(key, 1), (pair_total,), 1, per_group)
    split_flag = jax.random.randint(jax.random.fold_in(key, 2), (block_total,), 0, 2)
    split_flag = split_flag.at[0].set(0)
    cut_point = jax.random.randint(jax.random.fold_in(key, 3), (block_total,), 1, SHORT)
    position = jnp.arange(TOKENS, dtype=jnp.int32)
    group_of = position // TOK_G
    block_of = position // SHORT
    in_block = position % SHORT
    within = position % TOK_G // SHORT
    pair_of = group_of // 2
    tail_here = long_tail[pair_of]
    is_long = jnp.where(group_of % 2 == 0, within >= per_group - tail_here, within < per_group - tail_here)
    long_end = (2 * pair_of + 1) * TOK_G + (per_group - tail_here) * SHORT - 1
    block_start = block_of * SHORT
    cut_here = cut_point[block_of]
    short_end = jnp.where((split_flag[block_of] == 1) & (in_block < cut_here), block_start + cut_here - 1, block_start + SHORT - 1)
    return jnp.where(is_long, long_end, short_end).astype(jnp.int32)


def levels(rng, dims, pieces, least, high):
    level, own = 1.0, jax.random.fold_in(rng, 6)
    for dim, blocks in pieces:
        heights = jnp.exp(jax.random.uniform(jax.random.fold_in(own, dim), (blocks,), jnp.float32, least / len(pieces), high / len(pieces)))
        level = level * jnp.repeat(heights, dims[dim] // blocks).reshape([-1 if axis == dim else 1 for axis in range(len(dims))])
    return level


def gaussian(rng, extent, width, most, shards=(), kind=jnp.bfloat16):
    entries = jax.random.normal(rng, extent, jnp.float32) * width
    if len(shards) > 0:
        entries = levels(rng, extent, shards, -0.22, 0.18) * entries
    return jnp.clip(entries, min=-most, max=most).astype(kind)


def setup_inputs(seed: int = 0) -> dict:
    key_list = jax.random.split(jax.random.key(seed), 11)
    return {
        "hidden_in": draw_hidden_in(jax.random.fold_in(key_list[10], 71), 0),
        "request_ids": draw_request_ids(jax.random.fold_in(key_list[10], 71), 0),
        "w_qkv": draw_w_qkv(jax.random.fold_in(key_list[10], 71), 0),
        "w_out": gaussian(key_list[3], (D, D), D ** -0.5, 0.1875, ((0, 128),), jnp.float32),
        "w_up": gaussian(key_list[4], (D, FF), D ** -0.5, 0.1875, ((0, 128),), jnp.float32),
        "w_down": gaussian(key_list[5], (D, FF), FF ** -0.5, 0.09375, ((0, 128),), jnp.float32),
        "ln1_gain": jnp.clip(1.0 + 0.15 * jax.random.normal(key_list[6], (D,), jnp.float32), 0.25, 1.75),
        "ln1_shift": gaussian(key_list[7], (D,), 0.5, 3.0, (), jnp.float32),
        "ln2_gain": jnp.clip(1.0 + 0.15 * jax.random.normal(key_list[8], (D,), jnp.float32), 0.25, 1.75),
        "ln2_shift": gaussian(key_list[9], (D,), 0.5, 3.0, (), jnp.float32),
    }


def layer_norm(values_in, norm_gain, norm_shift):
    center = values_in - lax.optimization_barrier(jnp.mean(values_in, axis=-1, keepdims=True))
    spread = lax.optimization_barrier(jnp.mean(center * center, axis=-1, keepdims=True))
    return center * lax.rsqrt(spread + 1e-05) * norm_gain + norm_shift

def reference(hidden_in, request_ids, w_qkv, w_out, w_up, w_down, ln1_gain, ln1_shift, ln2_gain, ln2_shift):
    qkv_weight = w_qkv.astype(jnp.bfloat16)
    out_weight = w_out.astype(jnp.bfloat16)
    up_weight = w_up.astype(jnp.bfloat16)
    down_weight = w_down.astype(jnp.bfloat16)
    projected = jnp.dot(hidden_in, qkv_weight, preferred_element_type=jnp.float32)
    queries, key_rows, value_rows = lax.optimization_barrier((projected[:, :D].astype(jnp.bfloat16), projected[:, D:2 * D].astype(jnp.bfloat16), projected[:, 2 * D:].astype(jnp.bfloat16)))
    pair_count = N_GROUP // 2
    pair_span = 2 * TOK_G

    def pair_attend(pair_block):
        pair_queries, pair_keys, pair_values, pair_ids = pair_block
        heads_q = pair_queries.astype(jnp.float32).reshape(pair_span, HEADS, HD)
        heads_k = pair_keys.astype(jnp.float32).reshape(pair_span, HEADS, HD)
        heads_v = pair_values.astype(jnp.float32).reshape(pair_span, HEADS, HD)
        scores = jnp.einsum('qhd,khd->hqk', heads_q, heads_k) * HD ** (-0.5)
        allowed = pair_ids[:, None] == pair_ids[None, :]
        scores = jnp.where(allowed[None], scores, -1e+30)
        row_peak = lax.optimization_barrier(jnp.max(scores, axis=-1, keepdims=True))
        weights = lax.optimization_barrier(jnp.exp(scores - row_peak).astype(jnp.bfloat16)).astype(jnp.float32)
        totals = lax.optimization_barrier(jnp.sum(weights, axis=-1))
        mixed_heads = jnp.einsum('hqk,khd->qhd', weights, heads_v) / jnp.transpose(totals)[:, :, None]
        return mixed_heads.astype(jnp.bfloat16).reshape(pair_span, D)
    attended = lax.map(pair_attend, (queries.reshape(pair_count, pair_span, D), key_rows.reshape(pair_count, pair_span, D), value_rows.reshape(pair_count, pair_span, D), request_ids.reshape(pair_count, pair_span))).reshape(TOKENS, D)
    attn_sum = jnp.dot(attended, out_weight.T, preferred_element_type=jnp.float32)
    attn_normed = layer_norm(hidden_in.astype(jnp.float32) + attn_sum, ln1_gain, ln1_shift).astype(jnp.bfloat16)
    activated = jax.nn.gelu(jnp.dot(attn_normed, up_weight, preferred_element_type=jnp.float32), approximate=False).astype(jnp.bfloat16)
    feed_sum = jnp.dot(activated, down_weight.T, preferred_element_type=jnp.float32)
    output_rows = layer_norm(attn_normed.astype(jnp.float32) + feed_sum, ln2_gain, ln2_shift).astype(jnp.bfloat16)
    return (output_rows, key_rows, value_rows)
```

```python
import jax
import jax.numpy as jnp
from jax import lax
from jax.experimental import pallas as pl
from jax.experimental.pallas import tpu as pltpu
from jax.sharding import Mesh
from jax.sharding import PartitionSpec as P

HD = 64
BF = jnp.bfloat16
F32 = jnp.float32
EPS = 1e-05
NT = (((1,), (1,)), ((), ()))
GROUP = ("yh", "xx", "cc")
PART = ("zz", "yl")
PARAMS = pltpu.CompilerParams(vmem_limit_bytes=56 * 1024 * 1024)
VM = pl.BlockSpec(memory_space=pltpu.VMEM)
SM = pl.BlockSpec(memory_space=pltpu.SMEM)


def low_lanes(shape):
    return lax.broadcasted_iota(jnp.int32, shape, len(shape) - 1) < HD


def turned(value):
    return pltpu.roll(value, HD, len(value.shape) - 1)


def pack_kernel(qkv_ref, out_ref, up_ref, down_ref, packed_ref):
    rows, width = out_ref.shape
    copies, targets = packed_ref.shape[:2]
    shards = targets // 2
    hidden = up_ref.shape[1] // shards
    half_w, half_h = width // 2, hidden // 2
    low = low_lanes((rows, 128))
    for core in range(2):
        outs = []
        for pair in range(shards // 2):
            one = out_ref[:, pair * 256 : pair * 256 + 128]
            two = out_ref[:, pair * 256 + 128 : pair * 256 + 256]
            if core == 0:
                outs.append(jnp.where(low, one, turned(two)))
            else:
                outs.append(jnp.where(low, turned(one), two))
        out_half = jnp.concatenate(outs, axis=1).astype(BF)
        for part in range(shards):
            q_tile = qkv_ref[:, part * 128 : part * 128 + 128]
            k_tile = qkv_ref[:, width + part * 128 : width + part * 128 + 128]
            v_tile = qkv_ref[:, 2 * width + part * 128 : 2 * width + part * 128 + 128]
            if core == 0:
                qk = jnp.where(low, q_tile, turned(k_tile))
                vz = jnp.where(low, v_tile, 0.0)
            else:
                qk = jnp.where(low, turned(q_tile), k_tile)
                vz = jnp.where(low, turned(v_tile), 0.0)
            start = part * hidden + core * half_h
            up_half = up_ref[:, start : start + half_h].astype(BF)
            down_half = down_ref[:, start : start + half_h].astype(BF)
            row = jnp.concatenate([out_half, up_half, down_half, qk.astype(BF), vz.astype(BF)], axis=1)
            for copy in range(copies):
                packed_ref[copy, core * shards + part] = row


def attend_kernel(core_ref, own_ref, other_ref, weight_ref, idc_ref, idr_ref, att_ref, kv_own_ref, kv_other_ref, q_scr, k_scr, v_scr):
    core = core_ref[0]
    rows = own_ref.shape[0]
    shards = att_ref.shape[1]
    weight = weight_ref[...]
    low = low_lanes((rows, 128))
    for side, (x_ref, kv_ref) in enumerate(((own_ref, kv_own_ref), (other_ref, kv_other_ref))):
        projected = jnp.dot(x_ref[...], weight, preferred_element_type=F32)
        projected = projected.astype(BF).astype(F32)
        qk = projected[:, :128]
        vv = projected[:, 128:]
        keys = turned(qk)
        span = slice(side * rows, (side + 1) * rows)
        q_scr[span] = jnp.where(low, qk * (HD ** (-0.5)), 0.0).astype(BF)
        k_scr[span] = keys.astype(BF)
        v_scr[span] = jnp.where(low, vv, 1.0).astype(BF)
        kv_ref[...] = jnp.where(low, keys, turned(vv)).astype(BF)
    all_keys = k_scr[...]
    all_values = v_scr[...]
    ids_row = idr_ref[...]
    step = 128
    low_step = low_lanes((step, 128))

    def chunk(start):
        scores = lax.dot_general(q_scr[start : start + step], all_keys, NT, preferred_element_type=F32)
        same = idc_ref[start : start + step, 0:1] == ids_row
        scores = jnp.where(same, scores, -1e30)
        peak = jnp.max(scores, axis=1, keepdims=True)
        weights = jnp.exp(scores - peak).astype(BF)
        mixed = jnp.dot(weights, all_values, preferred_element_type=F32)
        return mixed / mixed[:, HD : HD + 1]

    for side in range(2):
        place = core if side == 0 else 1 - core
        for begin in range(0, rows // 2, step):
            first = chunk(side * rows + begin)
            second = chunk(side * rows + rows // 2 + begin)
            packed = jnp.where(low_step, first, turned(second)).astype(BF)
            for part in range(shards):
                att_ref[place, part, begin : begin + step] = packed


def normed(values, gain, shift):
    center = values - jnp.mean(values, axis=-1, keepdims=True)
    spread = jnp.mean(center * center, axis=-1, keepdims=True)
    return center * lax.rsqrt(spread + EPS) * gain + shift


def gelu(value):
    return 0.5 * value * (1.0 + lax.erf(value * (2.0 ** (-0.5))))


def feed_kernel(place_ref, att_ref, mine_ref, theirs_ref, x_ref, gain_ref, shift_ref, part_ref, keep_ref, att_scr, norm_scr):
    core = place_ref[0]
    part = place_ref[1]
    shards = att_ref.shape[1]
    half_rows = att_ref.shape[2]
    rows, width = x_ref.shape
    half_w = width // 2
    half_h = (mine_ref.shape[1] - 256 - half_w) // 2
    low = low_lanes((half_rows, 128))
    for side in range(2):
        place = core if side == 0 else 1 - core
        for pair in range(shards // 2):
            one = att_ref[place, 2 * pair].astype(F32)
            two = att_ref[place, 2 * pair + 1].astype(F32)
            lanes = slice(pair * 128, pair * 128 + 128)
            att_scr[side, :half_rows, lanes] = jnp.where(low, one, turned(two)).astype(BF)
            att_scr[side, half_rows:, lanes] = jnp.where(low, turned(one), two).astype(BF)
    gain = gain_ref[...]
    shift = shift_ref[...]
    step = rows // 2
    share = rows // shards
    for begin in range(0, rows, step):
        span = slice(begin, begin + step)
        total = x_ref[span].astype(F32)
        for side, ref in enumerate((mine_ref, theirs_ref)):
            total += lax.dot_general(att_scr[side, span], ref[:, :half_w], NT, preferred_element_type=F32)
        norm = normed(total, gain, shift).astype(BF)
        norm_scr[span] = norm
        result = jnp.zeros((step, width), F32)
        for ref in (mine_ref, theirs_ref):
            up = jnp.dot(norm, ref[:, half_w : half_w + half_h], preferred_element_type=F32)
            active = gelu(up).astype(BF)
            result += lax.dot_general(active, ref[:, half_w + half_h : half_w + 2 * half_h], NT, preferred_element_type=F32)
        for row in range(0, step, share):
            part_ref[(begin + row) // share] = result[row : row + share].astype(BF)
    keep_ref[...] = norm_scr[pl.ds(pl.multiple_of(part * share, share), share)]


def final_kernel(sums_ref, keep_ref, gain_ref, shift_ref, out_ref):
    total = keep_ref[...].astype(F32)
    for shard in range(sums_ref.shape[0]):
        total += sums_ref[shard].astype(F32)
    out_ref[...] = normed(total, gain_ref[...], shift_ref[...]).astype(BF)


def cache_kernel(core_ref, own_ref, got_ref, keys_ref, values_ref):
    low = low_lanes(own_ref.shape)
    own = own_ref[...].astype(F32)
    got = got_ref[...].astype(F32)
    even = core_ref[0] == 0
    first = jnp.where(even, own, got)
    second = jnp.where(even, got, own)
    keys_ref[...] = jnp.where(low, first, turned(second)).astype(BF)
    values_ref[...] = jnp.where(low, turned(first), second).astype(BF)


def exchange(value, axes):
    return lax.all_to_all(value, axes, split_axis=0, concat_axis=0, tiled=True)


def swapped(value):
    return lax.ppermute(value, "cc", [(0, 1), (1, 0)])


def body(hidden_in, request_ids, w_qkv, w_out, w_up, w_down, ln1_gain, ln1_shift, ln2_gain, ln2_shift):
    groups = lax.axis_size("yh") * lax.axis_size("xx") * lax.axis_size("cc")
    shards = lax.axis_size("zz") * lax.axis_size("yl")
    rows, width = hidden_in.shape
    part_rows = w_qkv.shape[0]
    hidden = w_up.shape[1] // shards
    columns = width // 2 + hidden + 256
    core = lax.axis_index("cc")
    part = lax.axis_index("zz") * lax.axis_size("yl") + lax.axis_index("yl")
    core_arg = core.reshape(1).astype(jnp.int32)
    place_arg = jnp.stack([core, part]).astype(jnp.int32)

    packed = pl.pallas_call(
        pack_kernel,
        out_shape=jax.ShapeDtypeStruct((groups // 2, 2 * shards, part_rows, columns), BF),
        in_specs=[VM] * 4,
        out_specs=VM,
        compiler_params=PARAMS,
        name="pack",
    )(w_qkv, w_out, w_up, w_down)
    served = exchange(packed.reshape(groups * shards, part_rows, columns), GROUP + PART)
    served = served.reshape(width, columns)
    other_hidden = swapped(hidden_in)
    other_ids = swapped(request_ids)
    ids = jnp.concatenate([request_ids, other_ids])
    ids_col = jnp.broadcast_to(ids[:, None], (2 * rows, 128))
    ids_row = ids[None, :]
    last = columns // 256 - 1

    att, kv_own, kv_other = pl.pallas_call(
        attend_kernel,
        grid=(1,),
        out_shape=(
            jax.ShapeDtypeStruct((2, shards, rows // 2, 128), BF),
            jax.ShapeDtypeStruct((rows, 128), BF),
            jax.ShapeDtypeStruct((rows, 128), BF),
        ),
        in_specs=[SM, VM, VM, pl.BlockSpec((width, 256), lambda i: (0, last)), VM, VM],
        out_specs=(VM, VM, VM),
        scratch_shapes=[pltpu.VMEM((2 * rows, 128), BF)] * 3,
        compiler_params=PARAMS,
        name="attend",
    )(core_arg, hidden_in, other_hidden, served, ids_col, ids_row)
    served_other = swapped(served)
    kv_got = swapped(kv_other)
    att_all = exchange(att.reshape(2 * shards, rows // 2, 128), ("cc",) + PART)
    att_all = att_all.reshape(2, shards, rows // 2, 128)

    keys_out, values_out = pl.pallas_call(
        cache_kernel,
        out_shape=(jax.ShapeDtypeStruct((rows, 128), BF),) * 2,
        in_specs=[SM, VM, VM],
        out_specs=(VM, VM),
        compiler_params=PARAMS,
        name="cache",
    )(core_arg, kv_own, kv_got)

    share = rows // shards
    sums, keep = pl.pallas_call(
        feed_kernel,
        out_shape=(
            jax.ShapeDtypeStruct((shards, share, width), BF),
            jax.ShapeDtypeStruct((share, width), BF),
        ),
        in_specs=[SM] + [VM] * 6,
        out_specs=(VM, VM),
        scratch_shapes=[pltpu.VMEM((2, rows, width // 2), BF), pltpu.VMEM((rows, width), BF)],
        compiler_params=PARAMS,
        name="feed",
    )(place_arg, att_all, served, served_other, hidden_in, ln1_gain[None, :], ln1_shift[None, :])
    sums_all = exchange(sums, PART)
    final = pl.pallas_call(
        final_kernel,
        out_shape=jax.ShapeDtypeStruct((share, width), BF),
        in_specs=[VM] * 4,
        out_specs=VM,
        compiler_params=PARAMS,
        name="final",
    )(sums_all, keep, ln2_gain[None, :], ln2_shift[None, :])
    return (final, keys_out, values_out)


def solution(mesh):
    fine = Mesh(mesh.devices.reshape(2, 4, 2, 4, 2), GROUP + PART)
    in_specs = (
        P(GROUP, None),
        P(GROUP),
        P(GROUP + PART, None),
        P(GROUP + PART, None),
        P(GROUP + PART, None),
        P(GROUP + PART, None),
        P(),
        P(),
        P(),
        P(),
    )
    out_specs = (P(GROUP + PART, None), P(GROUP, PART), P(GROUP, PART))
    return jax.shard_map(body, mesh=fine, in_specs=in_specs, out_specs=out_specs, check_vma=False)
```

```python
import jax
import jax.numpy as jnp
from jax import lax
from jax.experimental import pallas as pl
from jax.experimental.pallas import tpu as pltpu
from jax.sharding import Mesh
from jax.sharding import PartitionSpec as P

HD = 64
BF = jnp.bfloat16
F32 = jnp.float32
EPS = 1e-05
NT = (((1,), (1,)), ((), ()))
GROUP = ("yh", "xx", "cc")
PART = ("zz", "yl")
PARAMS = pltpu.CompilerParams(vmem_limit_bytes=24 * 1024 * 1024)
VM = pl.BlockSpec(memory_space=pltpu.VMEM)
SM = pl.BlockSpec(memory_space=pltpu.SMEM)


def low_lanes(shape):
    return lax.broadcasted_iota(jnp.int32, shape, len(shape) - 1) < HD


def turned(value):
    return pltpu.roll(value, HD, len(value.shape) - 1)


def pack_qkv_kernel(qkv_ref, packed_ref):
    rows = qkv_ref.shape[0]
    width = qkv_ref.shape[1] // 3
    copies, targets = packed_ref.shape[:2]
    shards = targets // 2
    low = low_lanes((rows, 128))
    for part in range(shards):
        q_tile = qkv_ref[:, part * 128 : part * 128 + 128]
        k_tile = qkv_ref[:, width + part * 128 : width + part * 128 + 128]
        v_tile = qkv_ref[:, 2 * width + part * 128 : 2 * width + part * 128 + 128]
        for core in range(2):
            if core == 0:
                qk = jnp.where(low, q_tile, turned(k_tile))
                vz = jnp.where(low, v_tile, 0.0)
            else:
                qk = jnp.where(low, turned(q_tile), k_tile)
                vz = jnp.where(low, turned(v_tile), 0.0)
            row = jnp.concatenate([qk.astype(BF), vz.astype(BF)], axis=1)
            for copy in range(copies):
                packed_ref[copy, core * shards + part] = row


def pack_rest_kernel(out_ref, up_ref, down_ref, packed_ref):
    width = out_ref.shape[1]
    copies, targets = packed_ref.shape[:2]
    shards = targets // 2
    hidden = up_ref.shape[1] // shards
    half_w, half_h = width // 2, hidden // 2
    for core in range(2):
        out_half = out_ref[:, core * half_w : core * half_w + half_w].astype(BF)
        for part in range(shards):
            start = part * hidden + core * half_h
            up_half = up_ref[:, start : start + half_h].astype(BF)
            down_half = down_ref[:, start : start + half_h].astype(BF)
            row = jnp.concatenate([out_half, up_half, down_half], axis=1)
            for copy in range(copies):
                packed_ref[copy, core * shards + part] = row


def attend_kernel(own_ref, other_ref, weight_ref, idc_ref, idr_ref, att_ref, kv_ref, send_ref, q_scr, k_scr, v_scr):
    rows = own_ref.shape[0]
    half = rows // 2
    weight = weight_ref[...]
    low = low_lanes((rows, 128))
    for side, x_ref in enumerate((own_ref, other_ref)):
        projected = jnp.dot(x_ref[...], weight, preferred_element_type=F32)
        projected = projected.astype(BF).astype(F32)
        qk = projected[:, :128]
        vv = projected[:, 128:]
        keys = turned(qk)
        span = slice(side * rows, (side + 1) * rows)
        q_scr[span] = jnp.where(low, qk * (HD ** (-0.5)), 0.0).astype(BF)
        k_scr[span] = keys.astype(BF)
        v_scr[span] = jnp.where(low, vv, 1.0).astype(BF)
        both = jnp.where(low, keys, turned(vv)).astype(BF)
        if side == 0:
            kv_ref[...] = both
        else:
            send_ref[half:] = both
    all_keys = k_scr[...]
    all_values = v_scr[...]
    ids_row = idr_ref[...]
    step = 128
    low_step = low_lanes((step, 128))

    def chunk(start):
        scores = lax.dot_general(q_scr[start : start + step], all_keys, NT, preferred_element_type=F32)
        same = idc_ref[start : start + step, 0:1] == ids_row
        scores = jnp.where(same, scores, -1e30)
        peak = jnp.max(scores, axis=1, keepdims=True)
        weights = jnp.exp(scores - peak).astype(BF)
        mixed = jnp.dot(weights, all_values, preferred_element_type=F32)
        return mixed / mixed[:, HD : HD + 1]

    for side in range(2):
        for begin in range(0, half, step):
            first = chunk(side * rows + begin)
            second = chunk(side * rows + half + begin)
            packed = jnp.where(low_step, first, turned(second)).astype(BF)
            if side == 0:
                att_ref[begin : begin + step] = packed
            else:
                send_ref[begin : begin + step] = packed


def join_kernel(core_ref, own_ref, got_ref, both_ref):
    half = own_ref.shape[0]
    low = low_lanes(own_ref.shape)
    own = own_ref[...].astype(F32)
    got = got_ref[:half].astype(F32)
    even = core_ref[0] == 0
    first = jnp.where(even, own, got)
    second = jnp.where(even, got, own)
    both_ref[:half] = jnp.where(low, first, turned(second)).astype(BF)
    both_ref[half:] = jnp.where(low, turned(first), second).astype(BF)


def normed(values, gain, shift):
    center = values - jnp.mean(values, axis=-1, keepdims=True)
    spread = jnp.mean(center * center, axis=-1, keepdims=True)
    return center * lax.rsqrt(spread + EPS) * gain + shift


def gelu(value):
    return 0.5 * value * (1.0 + lax.erf(value * (2.0 ** (-0.5))))


def feed_kernel(place_ref, *refs):
    (*piece_refs, mine_ref, theirs_ref, x_ref, gain_ref, shift_ref, part_ref, keep_ref, att_scr, norm_scr) = refs
    core = place_ref[0]
    part = place_ref[1]
    shards = len(piece_refs)
    rows, width = x_ref.shape
    half_w = width // 2
    half_h = (mine_ref.shape[1] - half_w) // 2
    for index, piece_ref in enumerate(piece_refs):
        source = part ^ index
        lanes = pl.ds(pl.multiple_of(source % (shards // 2) * 128, 128), 128)
        att_scr[source // (shards // 2), :, lanes] = piece_ref[...]
    gain = gain_ref[...]
    shift = shift_ref[...]
    step = rows // 2
    share = rows // shards
    for begin in range(0, rows, step):
        span = slice(begin, begin + step)
        total = x_ref[span].astype(F32)
        for side, ref in ((core, mine_ref), (1 - core, theirs_ref)):
            total += lax.dot_general(att_scr[side, span], ref[:, :half_w], NT, preferred_element_type=F32)
        norm = normed(total, gain, shift).astype(BF)
        norm_scr[span] = norm
        result = jnp.zeros((step, width), F32)
        for ref in (mine_ref, theirs_ref):
            up = jnp.dot(norm, ref[:, half_w : half_w + half_h], preferred_element_type=F32)
            active = gelu(up).astype(BF)
            result += lax.dot_general(active, ref[:, half_w + half_h : half_w + 2 * half_h], NT, preferred_element_type=F32)
        for row in range(0, step, share):
            part_ref[(begin + row) // share] = result[row : row + share].astype(BF)
    keep_ref[...] = norm_scr[pl.ds(pl.multiple_of(part * share, share), share)]


def final_kernel(sums_ref, keep_ref, gain_ref, shift_ref, out_ref):
    total = keep_ref[...].astype(F32)
    for shard in range(sums_ref.shape[0]):
        total += sums_ref[shard].astype(F32)
    out_ref[...] = normed(total, gain_ref[...], shift_ref[...]).astype(BF)


def cache_kernel(core_ref, own_ref, got_ref, keys_ref, values_ref):
    low = low_lanes(own_ref.shape)
    own = own_ref[...].astype(F32)
    got = got_ref[got_ref.shape[0] - own.shape[0] :].astype(F32)
    even = core_ref[0] == 0
    first = jnp.where(even, own, got)
    second = jnp.where(even, got, own)
    keys_ref[...] = jnp.where(low, first, turned(second)).astype(BF)
    values_ref[...] = jnp.where(low, turned(first), second).astype(BF)


def exchange(value, axes):
    return lax.all_to_all(value, axes, split_axis=0, concat_axis=0, tiled=True)


def swapped(value):
    return lax.ppermute(value, "cc", [(0, 1), (1, 0)])


def crossed(value, bits, shards):
    return lax.ppermute(value, PART, [(i, i ^ bits) for i in range(shards)])


def body(hidden_in, request_ids, w_qkv, w_out, w_up, w_down, ln1_gain, ln1_shift, ln2_gain, ln2_shift):
    groups = lax.axis_size("yh") * lax.axis_size("xx") * lax.axis_size("cc")
    shards = lax.axis_size("zz") * lax.axis_size("yl")
    rows, width = hidden_in.shape
    part_rows = w_qkv.shape[0]
    hidden = w_up.shape[1] // shards
    columns = width // 2 + hidden
    core = lax.axis_index("cc")
    part = lax.axis_index("zz") * lax.axis_size("yl") + lax.axis_index("yl")
    place_arg = jnp.stack([core, part]).astype(jnp.int32)

    def call(kernel, name, out_shape, in_specs, work=0, **more):
        more["cost_estimate"] = pl.CostEstimate(flops=work, bytes_accessed=2**20, transcendentals=0)
        flat = isinstance(out_shape, tuple)
        out_specs = (VM,) * len(out_shape) if flat else VM
        return pl.pallas_call(kernel, out_shape=out_shape, in_specs=in_specs, out_specs=out_specs, compiler_params=PARAMS, name=name, **more)

    def shape(*dims):
        return jax.ShapeDtypeStruct(dims, BF)

    packed_qkv = call(pack_qkv_kernel, "pack_qkv", shape(groups // 2, 2 * shards, part_rows, 256), [VM])(w_qkv)
    served_qkv = exchange(packed_qkv.reshape(groups * shards, part_rows, 256), GROUP + PART).reshape(width, 256)
    other_hidden = swapped(hidden_in)
    other_ids = swapped(request_ids)
    w_out, w_up, w_down, other_hidden, other_ids = lax.optimization_barrier((w_out, w_up, w_down, other_hidden, other_ids))
    packed_rest = call(pack_rest_kernel, "pack_rest", shape(groups // 2, 2 * shards, part_rows, columns), [VM] * 3)(w_out, w_up, w_down)
    packed_rest, served_qkv = lax.optimization_barrier((packed_rest, served_qkv))
    served = exchange(packed_rest.reshape(groups * shards, part_rows, columns), GROUP + PART).reshape(width, columns)
    ids = jnp.concatenate([request_ids, other_ids])
    ids_col = jnp.broadcast_to(ids[:, None], (2 * rows, 128))
    ids_row = ids[None, :]

    att_own, kv_own, send = call(
        attend_kernel,
        "attend",
        (shape(rows // 2, 128), shape(rows, 128), shape(rows // 2 + rows, 128)),
        [VM] * 5,
        6 * 10**9,
        scratch_shapes=[pltpu.VMEM((2 * rows, 128), BF)] * 3,
    )(hidden_in, other_hidden, served_qkv, ids_col, ids_row)
    got = swapped(send)
    pieces = {0: call(join_kernel, "join", shape(rows, 128), [SM, VM, VM])(place_arg, att_own, got)}
    for bits in (1, 2, 4, 6):
        pieces[bits] = crossed(pieces[0], bits, shards)
    for bits in (2, 4, 6):
        pieces[1 ^ bits] = crossed(pieces[1], bits, shards)
    early = tuple(i for i in pieces if i != shards - 1)
    served, held = lax.optimization_barrier((served, tuple(pieces[i] for i in early)))
    pieces.update(zip(early, held))
    served_other = swapped(served)

    keys_out, values_out = call(cache_kernel, "cache", (shape(rows, 128),) * 2, [SM, VM, VM])(place_arg, kv_own, got)

    share = rows // shards
    sums, keep = call(
        feed_kernel,
        "feed",
        (shape(shards, share, width), shape(share, width)),
        [SM] + [VM] * (shards + 5),
        6 * 10**9,
        scratch_shapes=[pltpu.VMEM((2, rows, width // 2), BF), pltpu.VMEM((rows, width), BF)],
    )(place_arg, *(pieces[i] for i in range(shards)), served, served_other, hidden_in, ln1_gain[None, :], ln1_shift[None, :])
    sums_all = exchange(sums, PART)
    final = call(final_kernel, "final", shape(share, width), [VM] * 4)(sums_all, keep, ln2_gain[None, :], ln2_shift[None, :])
    return (final, keys_out, values_out)


def solution(mesh):
    fine = Mesh(mesh.devices.reshape(2, 4, 2, 4, 2), GROUP + PART)
    in_specs = (
        P(GROUP, None),
        P(GROUP),
        P(GROUP + PART, None),
        P(GROUP + PART, None),
        P(GROUP + PART, None),
        P(GROUP + PART, None),
        P(),
        P(),
        P(),
        P(),
    )
    out_specs = (P(GROUP + PART, None), P(GROUP, PART), P(GROUP, PART))
    return jax.shard_map(body, mesh=fine, in_specs=in_specs, out_specs=out_specs, check_vma=False)
```

```python
import jax
import jax.numpy as jnp
from jax import lax
from jax.experimental import pallas as pl
from jax.experimental.pallas import tpu as pltpu
from jax.sharding import Mesh
from jax.sharding import PartitionSpec as P

HD = 64
BF = jnp.bfloat16
F32 = jnp.float32
EPS = 1e-05
NT = (((1,), (1,)), ((), ()))
GROUP = ("yh", "xx", "cc")
PART = ("zz", "yl")
PARAMS = pltpu.CompilerParams(vmem_limit_bytes=24 * 1024 * 1024)
VM = pl.BlockSpec(memory_space=pltpu.VMEM)
SM = pl.BlockSpec(memory_space=pltpu.SMEM)


def low_lanes(shape):
    return lax.broadcasted_iota(jnp.int32, shape, len(shape) - 1) < HD


def turned(value):
    return pltpu.roll(value, HD, len(value.shape) - 1)


def spread():
    rows = lax.broadcasted_iota(jnp.int32, (128, 128), 0)
    cols = lax.broadcasted_iota(jnp.int32, (128, 128), 1)
    block, inner = cols // HD, cols % HD
    source = block * HD + inner % 32 // 8 * 16 + inner // 32 * 8 + inner % 8
    return jnp.where(rows == source, 1.0, 0.0)


def spread_rows(ref):
    moved = jnp.dot(ref[...], spread(), preferred_element_type=F32, precision=lax.Precision.HIGHEST)
    return jnp.concatenate([moved[i : i + 1] for i in range(ref.shape[0])], axis=1)


def pack_qkv_kernel(qkv_ref, packed_ref):
    rows = qkv_ref.shape[0]
    width = qkv_ref.shape[1] // 3
    copies, cores, depth, twins = packed_ref.shape[:4]
    low = low_lanes((rows, 128))

    def tile(kind, number):
        start = kind * width + number * 128
        return qkv_ref[:, start : start + 128]

    for z in range(depth):
        for core in range(cores):
            parts = []
            for twin in range(2):
                q_tile, k_tile = tile(0, 2 * z + twin), tile(1, 2 * z + twin)
                if core == 0:
                    parts.append(jnp.where(low, q_tile, turned(k_tile)))
                else:
                    parts.append(jnp.where(low, turned(q_tile), k_tile))
            one, two = tile(2, 2 * z), tile(2, 2 * z + 1)
            if core == 0:
                parts.append(jnp.where(low, one, turned(two)))
            else:
                parts.append(jnp.where(low, turned(one), two))
            row = jnp.concatenate(parts, axis=1).astype(BF)
            for copy in range(copies):
                for twin in range(twins):
                    packed_ref[copy, core, z, twin] = row


def pack_depth_kernel(place_ref, out_ref, up_ref, down_ref, *piece_refs):
    depth = len(piece_refs)
    width = out_ref.shape[1]
    span = up_ref.shape[1] // depth
    out_rows = out_ref[...].astype(BF)
    for bits, piece_ref in enumerate(piece_refs):
        start = pl.multiple_of((place_ref[1] ^ bits) * span, span)
        piece_ref[:, :width] = out_rows
        piece_ref[:, width : width + span] = up_ref[:, pl.ds(start, span)].astype(BF)
        piece_ref[:, width + span :] = down_ref[:, pl.ds(start, span)].astype(BF)


def pack_rest_kernel(place_ref, *refs):
    *piece_refs, packed_ref = refs
    copies, cores, twins, depth = packed_ref.shape[:4]
    half_w = packed_ref.shape[5] // 2
    half_h = half_w // 2
    width = 2 * half_w
    for bits, piece_ref in enumerate(piece_refs):
        z = place_ref[1] ^ bits
        for core in range(cores):
            for twin in range(twins):
                start = width + twin * 2 * half_h + core * half_h
                row = jnp.concatenate(
                    [
                        piece_ref[:, core * half_w : core * half_w + half_w],
                        piece_ref[:, start : start + half_h],
                        piece_ref[:, start + 2 * twins * half_h : start + 2 * twins * half_h + half_h],
                    ],
                    axis=1,
                )
                for copy in range(copies):
                    packed_ref[copy, core, twin, z] = row


def attend_kernel(place_ref, own_ref, other_ref, weight_ref, idc_ref, idr_ref, att_ref, kv_ref, send_ref, q_scr, k_scr, v_scr):
    rows = own_ref.shape[0]
    weight = weight_ref[...]
    low = low_lanes((rows, 128))
    first_twin = place_ref[2] == 0
    for side, x_ref in enumerate((own_ref, other_ref)):
        projected = jnp.dot(x_ref[...], weight, preferred_element_type=F32)
        projected = projected.astype(BF).astype(F32)
        vv = projected[:, 256:]
        span = slice(side * rows, (side + 1) * rows)
        v_scr[0, span] = jnp.where(low, vv, 1.0).astype(BF)
        v_scr[1, span] = jnp.where(low, 1.0, vv).astype(BF)
        cached = []
        for head in range(2):
            qk = projected[:, head * 128 : head * 128 + 128]
            keys = turned(qk)
            q_scr[head, span] = jnp.where(low, qk * (HD ** (-0.5)), 0.0).astype(BF)
            k_scr[head, span] = keys.astype(BF)
            cached.append(jnp.where(low, keys, vv if head else turned(vv)))
        both = jnp.where(first_twin, cached[0], cached[1]).astype(BF)
        if side == 0:
            kv_ref[...] = both
        else:
            send_ref[rows:] = both
    ids_row = idr_ref[...]
    step = 128
    low_step = low_lanes((step, 128))
    for start in range(0, 2 * rows, step):
        same = idc_ref[start : start + step, 0:1] == ids_row
        mixed = []
        for head in range(2):
            scores = lax.dot_general(q_scr[head, start : start + step], k_scr[head], NT, preferred_element_type=F32)
            scores = jnp.where(same, scores, -1e30)
            peak = jnp.max(scores, axis=1, keepdims=True)
            weights = jnp.exp(scores - peak).astype(BF)
            both = jnp.dot(weights, v_scr[head], preferred_element_type=F32)
            mixed.append(both / both[:, HD - head * HD : HD - head * HD + 1])
        packed = jnp.where(low_step, mixed[0], mixed[1]).astype(BF)
        if start < rows:
            att_ref[start : start + step] = packed
        else:
            send_ref[start - rows : start - rows + step] = packed


def join_kernel(place_ref, own_ref, got_ref, both_ref):
    rows = own_ref.shape[0]
    low = low_lanes(own_ref.shape)
    own = own_ref[...].astype(F32)
    got = got_ref[:rows].astype(F32)
    even = place_ref[0] == 0
    first = jnp.where(even, own, got)
    second = jnp.where(even, got, own)
    both_ref[:, :128] = jnp.where(low, first, turned(second)).astype(BF)
    both_ref[:, 128:] = jnp.where(low, turned(first), second).astype(BF)


def normed(values, gain, shift):
    center = values - jnp.mean(values, axis=-1, keepdims=True)
    spread = jnp.mean(center * center, axis=-1, keepdims=True)
    return center * lax.rsqrt(spread + EPS) * gain + shift


def gelu(value):
    return 0.5 * value * (1.0 + lax.erf(value * (2.0 ** (-0.5))))


def feed_kernel(place_ref, *refs):
    (*piece_refs, mine_ref, theirs_ref, x_ref, gain_ref, shift_ref, part_ref, keep_ref, att_scr, norm_scr, x_scr) = refs
    core = place_ref[0]
    depth = len(piece_refs)
    shards = part_ref.shape[0]
    part = place_ref[1] * (shards // depth) + place_ref[2]
    rows, width = x_ref.shape
    half_w = width // 2
    half_h = (mine_ref.shape[1] - half_w) // 2
    block = width // depth
    for bits, piece_ref in enumerate(piece_refs):
        source = place_ref[1] ^ bits
        lanes = pl.ds(pl.multiple_of(source % (depth // 2) * block, block), block)
        att_scr[source // (depth // 2), :, lanes] = piece_ref[...]
    moved = spread().astype(BF)
    for lane in range(0, width, 128):
        x_scr[:, lane : lane + 128] = jnp.dot(x_ref[:, lane : lane + 128], moved, preferred_element_type=F32)
    gain = spread_rows(gain_ref)
    shift = spread_rows(shift_ref)
    step = rows // 2
    share = rows // shards
    for begin in range(0, rows, step):
        span = slice(begin, begin + step)
        total = x_scr[span]
        for side, ref in ((core, mine_ref), (1 - core, theirs_ref)):
            total += lax.dot_general(att_scr[side, span], ref[:, :half_w], NT, preferred_element_type=F32)
        norm = normed(total, gain, shift).astype(BF)
        norm_scr[span] = norm
        result = jnp.zeros((step, width), F32)
        for ref in (mine_ref, theirs_ref):
            up = jnp.dot(norm, ref[:, half_w : half_w + half_h], preferred_element_type=F32)
            active = gelu(up).astype(BF)
            result += lax.dot_general(active, ref[:, half_w + half_h : half_w + 2 * half_h], NT, preferred_element_type=F32)
        for row in range(0, step, share):
            part_ref[(begin + row) // share] = result[row : row + share].astype(BF)
    keep_ref[...] = norm_scr[pl.ds(pl.multiple_of(part * share, share), share)]


def final_kernel(sums_ref, keep_ref, gain_ref, shift_ref, out_ref):
    total = keep_ref[...].astype(F32)
    for shard in range(sums_ref.shape[0]):
        total += sums_ref[shard].astype(F32)
    result = normed(total, spread_rows(gain_ref), spread_rows(shift_ref)).astype(BF)
    moved = spread().astype(BF)
    for lane in range(0, total.shape[1], 128):
        tile = lax.dot_general(result[:, lane : lane + 128], moved, NT, preferred_element_type=F32)
        out_ref[:, lane : lane + 128] = tile.astype(BF)


def cache_kernel(place_ref, own_ref, got_ref, keys_ref, values_ref):
    low = low_lanes(own_ref.shape)
    own = own_ref[...].astype(F32)
    got = got_ref[got_ref.shape[0] - own.shape[0] :].astype(F32)
    even = place_ref[0] == 0
    first = jnp.where(even, own, got)
    second = jnp.where(even, got, own)
    keys_ref[...] = jnp.where(low, first, turned(second)).astype(BF)
    values_ref[...] = jnp.where(low, turned(first), second).astype(BF)


def exchange(value, axes):
    return lax.all_to_all(value, axes, split_axis=0, concat_axis=0, tiled=True)


def swapped(value):
    return lax.ppermute(value, "cc", [(0, 1), (1, 0)])


def crossed(value, bits):
    return lax.ppermute(value, "zz", [(i, i ^ bits) for i in range(lax.axis_size("zz"))])


def body(hidden_in, request_ids, w_qkv, w_out, w_up, w_down, ln1_gain, ln1_shift, ln2_gain, ln2_shift):
    copies = lax.axis_size("yh") * lax.axis_size("xx")
    cores = lax.axis_size("cc")
    depth = lax.axis_size("zz")
    twins = lax.axis_size("yl")
    shards = depth * twins
    rows, width = hidden_in.shape
    part_rows = w_qkv.shape[0]
    hidden = w_up.shape[1] // shards
    columns = width // 2 + hidden
    place = jnp.stack([lax.axis_index("cc"), lax.axis_index("zz"), lax.axis_index("yl")]).astype(jnp.int32)

    def call(kernel, name, out_shape, in_specs, work=0, **more):
        more["cost_estimate"] = pl.CostEstimate(flops=work, bytes_accessed=2**20, transcendentals=0)
        flat = isinstance(out_shape, tuple)
        out_specs = (VM,) * len(out_shape) if flat else VM
        return pl.pallas_call(kernel, out_shape=out_shape, in_specs=in_specs, out_specs=out_specs, compiler_params=PARAMS, name=name, **more)

    def shape(*dims):
        return jax.ShapeDtypeStruct(dims, BF)

    packed_qkv = call(pack_qkv_kernel, "pack_qkv", shape(copies, cores, depth, twins, part_rows, 384), [VM])(w_qkv)
    served_qkv = exchange(packed_qkv.reshape(-1, part_rows, 384), GROUP + PART).reshape(width, 384)
    other_hidden = swapped(hidden_in)
    other_ids = swapped(request_ids)
    span = 2 * hidden * twins + width
    sent = call(pack_depth_kernel, "pack_depth", (shape(part_rows, span),) * depth, [SM] + [VM] * 3)(place, w_out, w_up, w_down)
    held = [sent[0]] + [crossed(sent[bits], bits) for bits in range(1, depth)]
    held, other_hidden, other_ids = lax.optimization_barrier((held, other_hidden, other_ids))
    packed_rest = call(pack_rest_kernel, "pack_rest", shape(copies, cores, twins, depth, part_rows, columns), [SM] + [VM] * depth)(place, *held)
    packed_rest, served_qkv = lax.optimization_barrier((packed_rest, served_qkv))
    served = exchange(packed_rest.reshape(-1, depth, part_rows, columns), GROUP + ("yl",)).reshape(width, columns)
    ids = jnp.concatenate([request_ids, other_ids])
    ids_col = jnp.broadcast_to(ids[:, None], (2 * rows, 128))
    ids_row = ids[None, :]

    att_own, kv_own, send = call(
        attend_kernel,
        "attend",
        (shape(rows, 128), shape(rows, 128), shape(2 * rows, 128)),
        [SM] + [VM] * 5,
        6 * 10**9,
        scratch_shapes=[pltpu.VMEM((2, 2 * rows, 128), BF)] * 3,
    )(place, hidden_in, other_hidden, served_qkv, ids_col, ids_row)
    got = swapped(send)
    pieces = [call(join_kernel, "join", shape(rows, 256), [SM, VM, VM])(place, att_own, got)]
    pieces += [crossed(pieces[0], bits) for bits in range(1, depth)]
    served, pieces = lax.optimization_barrier((served, pieces))
    served_other = swapped(served)

    keys_out, values_out = call(cache_kernel, "cache", (shape(rows, 128),) * 2, [SM, VM, VM])(place, kv_own, got)

    share = rows // shards
    tiles = (width // 128, 128)
    sums, keep = call(
        feed_kernel,
        "feed",
        (shape(shards, share, width), shape(share, width)),
        [SM] + [VM] * (depth + 5),
        6 * 10**9,
        scratch_shapes=[pltpu.VMEM((2, rows, width // 2), BF), pltpu.VMEM((rows, width), BF), pltpu.VMEM((rows, width), F32)],
    )(place, *pieces, served, served_other, hidden_in, ln1_gain.reshape(tiles), ln1_shift.reshape(tiles))
    sums_all = exchange(sums, PART)
    final = call(final_kernel, "final", shape(share, width), [VM] * 4)(sums_all, keep, ln2_gain.reshape(tiles), ln2_shift.reshape(tiles))
    return (final, keys_out, values_out)


def solution(mesh):
    fine = Mesh(mesh.devices.reshape(2, 4, 2, 4, 2), GROUP + PART)
    in_specs = (
        P(GROUP, None),
        P(GROUP),
        P(GROUP + PART, None),
        P(GROUP + PART, None),
        P(GROUP + PART, None),
        P(GROUP + PART, None),
        P(),
        P(),
        P(),
        P(),
    )
    out_specs = (P(GROUP + PART, None), P(GROUP, PART), P(GROUP, PART))
    return jax.shard_map(body, mesh=fine, in_specs=in_specs, out_specs=out_specs, check_vma=False)
```

```python
import jax
import jax.numpy as jnp
from jax import lax
from jax.experimental import pallas as pl
from jax.experimental.pallas import tpu as pltpu
from jax.sharding import Mesh
from jax.sharding import PartitionSpec as P

HD = 64
BF = jnp.bfloat16
F32 = jnp.float32
EPS = 1e-05
NT = (((1,), (1,)), ((), ()))
GROUP = ("yh", "xx", "cc")
PART = ("zz", "yl")
VM = pl.BlockSpec(memory_space=pltpu.VMEM)
SM = pl.BlockSpec(memory_space=pltpu.SMEM)
HB = pl.BlockSpec(memory_space=pltpu.HBM)
CORE, DEEP, TWIN = range(3)


def low_lanes(shape):
    return lax.broadcasted_iota(jnp.int32, shape, len(shape) - 1) < HD


def turned(value):
    return pltpu.roll(value, HD, len(value.shape) - 1)


def spread():
    rows = lax.broadcasted_iota(jnp.int32, (128, 128), 0)
    cols = lax.broadcasted_iota(jnp.int32, (128, 128), 1)
    inner = cols % 64
    source = cols - inner + inner % 32 // 8 * 16 + inner // 32 * 8 + inner % 8
    return jnp.where(rows == source, 1.0, 0.0).astype(BF)


def rearranged(value, back):
    moved = spread()
    tiles = []
    for lane in range(0, value.shape[1], 128):
        tile = value[:, lane : lane + 128]
        if back:
            tiles.append(lax.dot_general(tile, moved, NT, preferred_element_type=F32).astype(BF))
        else:
            tiles.append(jnp.dot(tile, moved, preferred_element_type=F32).astype(BF))
    return jnp.concatenate(tiles, axis=1)


def pack_first_kernel(qkv_ref, out_ref, packed_ref):
    rows = qkv_ref.shape[0]
    width = qkv_ref.shape[1] // 3
    copies, cores, depth, twins = packed_ref.shape[:4]
    low = low_lanes((rows, 128))

    def tile(kind, number):
        start = kind * width + number * 128
        return qkv_ref[:, start : start + 128]

    for core in range(cores):
        for z in range(depth):
            start = core * (width // cores) + z * 128
            parts = [out_ref[:, start : start + 128]]
            for twin in range(2):
                q_tile, k_tile = tile(0, 2 * z + twin), tile(1, 2 * z + twin)
                if core == 0:
                    parts.append(jnp.where(low, q_tile, turned(k_tile)))
                else:
                    parts.append(jnp.where(low, turned(q_tile), k_tile))
            one, two = tile(2, 2 * z), tile(2, 2 * z + 1)
            if core == 0:
                parts.append(jnp.where(low, one, turned(two)))
            else:
                parts.append(jnp.where(low, turned(one), two))
            row = jnp.concatenate(parts, axis=1).astype(BF)
            for copy in range(copies):
                for twin in range(twins):
                    packed_ref[copy, core, z, twin] = row


def pack_depth_kernel(place_ref, up_ref, down_ref, *piece_refs):
    depth = len(piece_refs)
    span = up_ref.shape[1] // depth
    for bits, piece_ref in enumerate(piece_refs):
        start = pl.multiple_of((place_ref[DEEP] ^ bits) * span, span)
        piece_ref[:, :span] = up_ref[:, pl.ds(start, span)].astype(BF)
        piece_ref[:, span:] = down_ref[:, pl.ds(start, span)].astype(BF)


def pack_rest_kernel(place_ref, *refs):
    *piece_refs, packed_ref = refs
    copies, cores, twins = packed_ref.shape[:3]
    half_h = packed_ref.shape[5] // 2
    for bits, piece_ref in enumerate(piece_refs):
        z = place_ref[DEEP] ^ bits
        span = piece_ref.shape[1] // 2
        for core in range(cores):
            start = core * half_h
            row = jnp.concatenate([piece_ref[:, start : start + half_h], piece_ref[:, span + start : span + start + half_h]], axis=1)
            for copy in range(copies):
                for twin in range(twins):
                    packed_ref[copy, core, twin, z] = row


def take_kernel(served_ref, part_ref):
    part_ref[...] = served_ref[...]


def assemble_kernel(place_ref, *refs):
    *part_refs, whole_ref = refs
    for bits, part_ref in enumerate(part_refs):
        lanes = pl.ds(pl.multiple_of((place_ref[DEEP] ^ bits) * 128, 128), 128)
        whole_ref[:, lanes] = part_ref[...]


def attend_kernel(place_ref, own_hbm, other_hbm, weight_ref, own_ids_ref, other_ids_ref, att_ref, kv_ref, send_ref, x_scr, q_scr, k_scr, v_scr, id_scr, sems):
    copies = [pltpu.make_async_copy(ref, x_scr.at[side], sems.at[side]) for side, ref in enumerate((own_hbm, other_hbm))]
    for copy in copies:
        copy.start()
    rows = own_hbm.shape[0]
    step = 128
    tiles = rows // step
    share = att_ref.shape[0] // tiles
    twin = place_ref[TWIN]
    weight = weight_ref[:, 128:]
    low = low_lanes((rows, 128))
    for side, ids_ref in enumerate((own_ids_ref, other_ids_ref)):
        id_scr[side * tiles : (side + 1) * tiles] = ids_ref[...].astype(F32)
        copies[side].wait()
        projected = jnp.dot(x_scr[side], weight, preferred_element_type=F32)
        projected = projected.astype(BF).astype(F32)
        vv = projected[:, 256:]
        span = slice(side * rows, (side + 1) * rows)
        v_scr[0, span] = jnp.where(low, vv, 1.0).astype(BF)
        v_scr[1, span] = jnp.where(low, 1.0, vv).astype(BF)
        cached = []
        for head in range(2):
            qk = projected[:, head * 128 : head * 128 + 128]
            keys = turned(qk)
            q_scr[head, span] = jnp.where(low, qk * (HD ** (-0.5)), 0.0).astype(BF)
            k_scr[head, span] = keys.astype(BF)
            cached.append(jnp.where(low, keys, vv if head else turned(vv)))
        both = jnp.where(twin == 0, cached[0], cached[1]).astype(BF)
        if side == 0:
            kv_ref[...] = both
        else:
            send_ref[att_ref.shape[0] :] = both
    ids_row = jnp.concatenate([id_scr[i : i + 1] for i in range(2 * tiles)], axis=1)
    low_step = low_lanes((step, 128))
    row_at = lax.broadcasted_iota(jnp.int32, (step, 128), 0)
    lane_at = lax.broadcasted_iota(jnp.int32, (step, 128), 1)
    picked = lane_at == twin * share + row_at % share
    for side in range(2):
        for pair in range(tiles // 2):
            one = side * tiles + 2 * pair
            ids_two = jnp.where(row_at < share, id_scr[one : one + 1], id_scr[one + 1 : one + 2])
            ids_col = jnp.sum(jnp.where(picked, ids_two, 0.0), axis=1, keepdims=True)
            same = ids_col == ids_row
            spans = [pl.ds(pl.multiple_of((one + i) * step + twin * share, share), share) for i in range(2)]
            mixed = []
            for head in range(2):
                queries = jnp.concatenate([q_scr[head, span] for span in spans], axis=0)
                scores = lax.dot_general(queries, k_scr[head], NT, preferred_element_type=F32)
                scores = jnp.where(same, scores, -1e30)
                peak = jnp.max(scores, axis=1, keepdims=True)
                weights = jnp.exp(scores - peak).astype(BF)
                both = jnp.dot(weights, v_scr[head], preferred_element_type=F32)
                mixed.append(both / both[:, HD - head * HD : HD - head * HD + 1])
            packed = jnp.where(low_step, mixed[0], mixed[1]).astype(BF)
            ref = send_ref if side else att_ref
            ref[pair * step : (pair + 1) * step] = packed


def join_kernel(place_ref, own_ref, got_ref, both_ref):
    rows = own_ref.shape[0]
    low = low_lanes(own_ref.shape)
    own = own_ref[...].astype(F32)
    got = got_ref[:rows].astype(F32)
    even = place_ref[CORE] == 0
    first = jnp.where(even, own, got)
    second = jnp.where(even, got, own)
    both_ref[:, :128] = jnp.where(low, first, turned(second)).astype(BF)
    both_ref[:, 128:] = jnp.where(low, turned(first), second).astype(BF)


def normed(values, gain, shift):
    center = values - jnp.mean(values, axis=-1, keepdims=True)
    spread_out = jnp.mean(center * center, axis=-1, keepdims=True)
    return center * lax.rsqrt(spread_out + EPS) * gain + shift


def gelu(value):
    return 0.5 * value * (1.0 + lax.erf(value * (2.0 ** (-0.5))))


def project_kernel(place_ref, *refs):
    (*piece_refs, mine_ref, theirs_ref, x_hbm, gain_ref, shift_ref, norm_ref, keep_ref, att_scr, x_ref, sems) = refs
    depth = len(piece_refs)
    rows, width = norm_ref.shape
    share = rows // depth
    twins = x_hbm.shape[0] // rows
    copies = []
    for z in range(depth):
        start = pl.multiple_of((z * twins + place_ref[TWIN]) * share, share)
        copies.append(pltpu.make_async_copy(x_hbm.at[pl.ds(start, share)], x_ref.at[pl.ds(z * share, share)], sems.at[z]))
        copies[-1].start()
    core = place_ref[CORE]
    block = width // depth
    for bits, piece_ref in enumerate(piece_refs):
        source = place_ref[DEEP] ^ bits
        lanes = pl.ds(pl.multiple_of(source % (depth // 2) * block, block), block)
        att_scr[source // (depth // 2), :, lanes] = piece_ref[...]
    for copy in copies:
        copy.wait()
    total = x_ref[...].astype(F32)
    for side, ref in ((core, mine_ref), (1 - core, theirs_ref)):
        total += lax.dot_general(att_scr[side], ref[...], NT, preferred_element_type=F32)
    norm_ref[...] = normed(total, gain_ref[...], shift_ref[...]).astype(BF)
    keep_ref[...] = norm_ref[pl.ds(pl.multiple_of(place_ref[DEEP] * share, share), share)]


def feed_kernel(place_ref, norm_ref, mine_ref, theirs_ref, *refs):
    *sum_refs, sum_scr = refs
    half_h = mine_ref.shape[1] // 2
    share = sum_refs[0].shape[0]
    arrived = rearranged(norm_ref[...], False)
    result = jnp.zeros(norm_ref.shape, F32)
    for ref in (mine_ref, theirs_ref):
        up = jnp.dot(arrived, ref[:, :half_h], preferred_element_type=F32)
        active = gelu(up).astype(BF)
        result += lax.dot_general(active, ref[:, half_h:], NT, preferred_element_type=F32)
    sum_scr[...] = rearranged(result.astype(BF), True)
    for bits, sum_ref in enumerate(sum_refs):
        sum_ref[...] = sum_scr[pl.ds(pl.multiple_of((place_ref[DEEP] ^ bits) * share, share), share)]


def final_kernel(*refs):
    *sum_refs, keep_ref, gain_ref, shift_ref, out_ref = refs
    total = keep_ref[...].astype(F32)
    for sum_ref in sum_refs:
        total += sum_ref[...].astype(F32)
    out_ref[...] = normed(total, gain_ref[...], shift_ref[...]).astype(BF)


def cache_kernel(place_ref, own_ref, got_ref, keys_ref, values_ref):
    low = low_lanes(own_ref.shape)
    own = own_ref[...].astype(F32)
    got = got_ref[got_ref.shape[0] - own.shape[0] :].astype(F32)
    even = place_ref[CORE] == 0
    first = jnp.where(even, own, got)
    second = jnp.where(even, got, own)
    keys_ref[...] = jnp.where(low, first, turned(second)).astype(BF)
    values_ref[...] = jnp.where(low, turned(first), second).astype(BF)


def exchange(value, axes):
    return lax.all_to_all(value, axes, split_axis=0, concat_axis=0, tiled=True)


def swapped(value):
    return lax.ppermute(value, "cc", [(0, 1), (1, 0)])


def crossed(values):
    size = len(values)
    return [values[0]] + [lax.ppermute(values[bits], "zz", [(i, i ^ bits) for i in range(size)]) for bits in range(1, size)]


def body(hidden_in, request_ids, w_qkv, w_out, w_up, w_down, ln1_gain, ln1_shift, ln2_gain, ln2_shift):
    copies = lax.axis_size("yh") * lax.axis_size("xx")
    cores = lax.axis_size("cc")
    depth = lax.axis_size("zz")
    twins = lax.axis_size("yl")
    rows, width = hidden_in.shape
    unit = w_qkv.shape[0]
    hidden = w_up.shape[1] // depth
    place = jnp.stack([lax.axis_index("cc"), lax.axis_index("zz"), lax.axis_index("yl")]).astype(jnp.int32)

    def call(kernel, name, out_shape, in_specs, work=0, room=8, **more):
        more["cost_estimate"] = pl.CostEstimate(flops=work, bytes_accessed=2**20, transcendentals=0)
        flat = isinstance(out_shape, tuple)
        more.setdefault("out_specs", (VM,) * len(out_shape) if flat else VM)
        params = pltpu.CompilerParams(vmem_limit_bytes=room * 2**20)
        return pl.pallas_call(kernel, out_shape=out_shape, in_specs=in_specs, compiler_params=params, name=name, **more)

    def shape(*dims):
        return jax.ShapeDtypeStruct(dims, BF)

    first_cols = 128 + 384
    packed = call(pack_first_kernel, "pack_first", shape(copies, cores, depth, twins, unit, first_cols), [VM, VM])(w_qkv, w_out)
    served = exchange(packed.reshape(-1, unit, first_cols), GROUP + PART).reshape(width, first_cols)
    other_hidden = swapped(hidden_in)
    other_ids = swapped(request_ids)
    held = crossed(call(pack_depth_kernel, "pack_depth", (shape(unit, 2 * hidden),) * depth, [SM, VM, VM])(place, w_up, w_down))
    held, other_hidden, other_ids = lax.optimization_barrier((held, other_hidden, other_ids))
    packed_rest = call(pack_rest_kernel, "pack_rest", shape(copies, cores, twins, depth, unit, hidden), [SM] + [VM] * depth)(place, *held)
    packed_rest, served = lax.optimization_barrier((packed_rest, served))
    rest = exchange(packed_rest.reshape(-1, depth, unit, hidden), GROUP + ("yl",)).reshape(width, hidden)

    out_part = call(take_kernel, "take", shape(width, 128), [pl.BlockSpec((width, 128), lambda i: (0, 0))], grid=(1,), out_specs=pl.BlockSpec((width, 128), lambda i: (0, 0)))(served)
    out_parts = crossed([out_part] * depth)
    id_tiles = (rows // 128, 128)
    few = rows // twins
    att_own, kv_own, send = call(
        attend_kernel,
        "attend",
        (shape(few, 128), shape(rows, 128), shape(few + rows, 128)),
        [SM, HB, HB, VM, VM, VM],
        5 * 10**9,
        16,
        scratch_shapes=[pltpu.VMEM((2, rows, width), BF)]
        + [pltpu.VMEM((2, 2 * rows, 128), BF)] * 3
        + [pltpu.VMEM((2 * rows // 128, 128), F32), pltpu.SemaphoreType.DMA((2,))],
    )(place, hidden_in, other_hidden, served, request_ids.reshape(id_tiles), other_ids.reshape(id_tiles))
    got = swapped(send)
    joined = call(join_kernel, "join", shape(few, 256), [SM, VM, VM])(place, att_own, got)
    pieces = crossed([joined] * depth)
    rest, out_parts, pieces = lax.optimization_barrier((rest, out_parts, pieces))
    mine_out = call(assemble_kernel, "assemble", shape(width, width // cores), [SM] + [VM] * depth)(place, *out_parts)
    theirs_out = swapped(mine_out)
    theirs = swapped(rest)
    keys_out, values_out = call(cache_kernel, "cache", (shape(rows, 128),) * 2, [SM, VM, VM], 10**9)(place, kv_own, got)

    share = few // depth
    norm, keep = call(
        project_kernel,
        "project",
        (shape(few, width), shape(share, width)),
        [SM] + [VM] * (depth + 2) + [HB, VM, VM],
        2 * 10**9,
        16,
        scratch_shapes=[pltpu.VMEM((2, few, width // 2), BF), pltpu.VMEM((few, width), BF), pltpu.SemaphoreType.DMA((depth,))],
    )(place, *pieces, mine_out, theirs_out, hidden_in, ln1_gain[None, :], ln1_shift[None, :])
    sums = call(
        feed_kernel,
        "feed",
        (shape(share, width),) * depth,
        [SM] + [VM] * 3,
        3 * 10**9,
        20,
        scratch_shapes=[pltpu.VMEM((few, width), BF)],
    )(place, norm, rest, theirs)
    sums = crossed(sums)
    final = call(final_kernel, "final", shape(share, width), [VM] * (depth + 3))(*sums, keep, ln2_gain[None, :], ln2_shift[None, :])
    return (final, keys_out, values_out)


def solution(mesh):
    fine = Mesh(mesh.devices.reshape(2, 4, 2, 4, 2), GROUP + PART)
    in_specs = (
        P(GROUP, None),
        P(GROUP),
        P(GROUP + PART, None),
        P(GROUP + PART, None),
        P(GROUP + PART, None),
        P(GROUP + PART, None),
        P(),
        P(),
        P(),
        P(),
    )
    out_specs = (P(GROUP + PART, None), P(GROUP, PART), P(GROUP, PART))
    return jax.shard_map(body, mesh=fine, in_specs=in_specs, out_specs=out_specs, check_vma=False)
```

```python
import jax
import jax.numpy as jnp
from jax import lax
from jax.experimental import pallas as pl
from jax.experimental.pallas import tpu as pltpu
from jax.sharding import Mesh
from jax.sharding import PartitionSpec as P

HD = 64
BF = jnp.bfloat16
F32 = jnp.float32
EPS = 1e-05
NT = (((1,), (1,)), ((), ()))
GROUP = ("yh", "xx", "cc")
PART = ("zz", "yl")
VM = pl.BlockSpec(memory_space=pltpu.VMEM)
SM = pl.BlockSpec(memory_space=pltpu.SMEM)
HB = pl.BlockSpec(memory_space=pltpu.HBM)
CORE, DEEP, TWIN = range(3)


def low_lanes(shape):
    return lax.broadcasted_iota(jnp.int32, shape, len(shape) - 1) < HD


def turned(value):
    return pltpu.roll(value, HD, len(value.shape) - 1)


def spread():
    rows = lax.broadcasted_iota(jnp.int32, (128, 128), 0)
    cols = lax.broadcasted_iota(jnp.int32, (128, 128), 1)
    inner = cols % 64
    source = cols - inner + inner % 32 // 8 * 16 + inner // 32 * 8 + inner % 8
    return jnp.where(rows == source, 1.0, 0.0).astype(BF)


def rearranged(value, back):
    moved = spread()
    tiles = []
    for lane in range(0, value.shape[1], 128):
        tile = value[:, lane : lane + 128]
        if back:
            tiles.append(lax.dot_general(tile, moved, NT, preferred_element_type=F32).astype(BF))
        else:
            tiles.append(jnp.dot(tile, moved, preferred_element_type=F32).astype(BF))
    return jnp.concatenate(tiles, axis=1)


def pack_first_kernel(qkv_ref, out_ref, packed_ref):
    rows = qkv_ref.shape[0]
    width = qkv_ref.shape[1] // 3
    copies, cores, depth, twins = packed_ref.shape[:4]
    low = low_lanes((rows, 128))

    def tile(kind, number):
        start = kind * width + number * 128
        return qkv_ref[:, start : start + 128]

    for core in range(cores):
        for z in range(depth):
            start = core * (width // cores) + z * 128
            parts = [out_ref[:, start : start + 128]]
            for twin in range(2):
                q_tile, k_tile = tile(0, 2 * z + twin), tile(1, 2 * z + twin)
                if core == 0:
                    parts.append(jnp.where(low, q_tile, turned(k_tile)))
                else:
                    parts.append(jnp.where(low, turned(q_tile), k_tile))
            one, two = tile(2, 2 * z), tile(2, 2 * z + 1)
            if core == 0:
                parts.append(jnp.where(low, one, turned(two)))
            else:
                parts.append(jnp.where(low, turned(one), two))
            row = jnp.concatenate(parts, axis=1).astype(BF)
            for copy in range(copies):
                for twin in range(twins):
                    packed_ref[copy, core, z, twin] = row


def pack_depth_kernel(place_ref, up_ref, down_ref, *piece_refs):
    depth = len(piece_refs)
    span = up_ref.shape[1] // depth
    for bits, piece_ref in enumerate(piece_refs):
        start = pl.multiple_of((place_ref[DEEP] ^ bits) * span, span)
        piece_ref[:, :span] = up_ref[:, pl.ds(start, span)].astype(BF)
        piece_ref[:, span:] = down_ref[:, pl.ds(start, span)].astype(BF)


def pack_rest_kernel(place_ref, *refs):
    *piece_refs, packed_ref = refs
    copies, cores, twins = packed_ref.shape[:3]
    half_h = packed_ref.shape[5] // 2
    for bits, piece_ref in enumerate(piece_refs):
        z = place_ref[DEEP] ^ bits
        span = piece_ref.shape[1] // 2
        for core in range(cores):
            start = core * half_h
            row = jnp.concatenate([piece_ref[:, start : start + half_h], piece_ref[:, span + start : span + start + half_h]], axis=1)
            for copy in range(copies):
                for twin in range(twins):
                    packed_ref[copy, core, twin, z] = row


def take_kernel(served_ref, part_ref):
    part_ref[...] = served_ref[...]


def assemble_kernel(place_ref, *refs):
    *part_refs, whole_ref = refs
    for bits, part_ref in enumerate(part_refs):
        lanes = pl.ds(pl.multiple_of((place_ref[DEEP] ^ bits) * 128, 128), 128)
        whole_ref[:, lanes] = part_ref[...]


def attend_kernel(place_ref, own_hbm, other_hbm, weight_ref, own_ids_ref, other_ids_ref, att_ref, kv_ref, send_ref, x_scr, q_scr, k_scr, v_scr, id_scr, sems):
    copies = [pltpu.make_async_copy(ref, x_scr.at[side], sems.at[side]) for side, ref in enumerate((own_hbm, other_hbm))]
    for copy in copies:
        copy.start()
    rows = own_hbm.shape[0]
    step = 128
    tiles = rows // step
    share = att_ref.shape[0] // tiles
    twin = place_ref[TWIN]
    weight = weight_ref[:, 128:]
    low = low_lanes((rows, 128))
    for side, ids_ref in enumerate((own_ids_ref, other_ids_ref)):
        id_scr[side * tiles : (side + 1) * tiles] = ids_ref[...].astype(F32)
        copies[side].wait()
        projected = jnp.dot(x_scr[side], weight, preferred_element_type=F32)
        projected = projected.astype(BF).astype(F32)
        vv = projected[:, 256:]
        span = slice(side * rows, (side + 1) * rows)
        v_scr[0, span] = jnp.where(low, vv, 1.0).astype(BF)
        v_scr[1, span] = jnp.where(low, 1.0, vv).astype(BF)
        cached = []
        for head in range(2):
            qk = projected[:, head * 128 : head * 128 + 128]
            keys = turned(qk)
            q_scr[head, span] = jnp.where(low, qk * (HD ** (-0.5)), 0.0).astype(BF)
            k_scr[head, span] = keys.astype(BF)
            cached.append(jnp.where(low, keys, vv if head else turned(vv)))
        both = jnp.where(twin == 0, cached[0], cached[1]).astype(BF)
        if side == 0:
            kv_ref[...] = both
        else:
            send_ref[att_ref.shape[0] :] = both
    ids_row = jnp.concatenate([id_scr[i : i + 1] for i in range(2 * tiles)], axis=1)
    low_step = low_lanes((step, 128))
    row_at = lax.broadcasted_iota(jnp.int32, (step, 128), 0)
    lane_at = lax.broadcasted_iota(jnp.int32, (step, 128), 1)
    picked = lane_at == twin * share + row_at % share
    for side in range(2):
        for pair in range(tiles // 2):
            one = side * tiles + 2 * pair
            ids_two = jnp.where(row_at < share, id_scr[one : one + 1], id_scr[one + 1 : one + 2])
            ids_col = jnp.sum(jnp.where(picked, ids_two, 0.0), axis=1, keepdims=True)
            same = ids_col == ids_row
            spans = [pl.ds(pl.multiple_of((one + i) * step + twin * share, share), share) for i in range(2)]
            mixed = []
            for head in range(2):
                queries = jnp.concatenate([q_scr[head, span] for span in spans], axis=0)
                scores = lax.dot_general(queries, k_scr[head], NT, preferred_element_type=F32)
                scores = jnp.where(same, scores, -1e30)
                peak = jnp.max(scores, axis=1, keepdims=True)
                weights = jnp.exp(scores - peak).astype(BF)
                both = jnp.dot(weights, v_scr[head], preferred_element_type=F32)
                mixed.append(both / both[:, HD - head * HD : HD - head * HD + 1])
            packed = jnp.where(low_step, mixed[0], mixed[1]).astype(BF)
            ref = send_ref if side else att_ref
            ref[pair * step : (pair + 1) * step] = packed


def join_kernel(place_ref, own_ref, got_ref, both_ref):
    rows = own_ref.shape[0]
    low = low_lanes(own_ref.shape)
    own = own_ref[...].astype(F32)
    got = got_ref[:rows].astype(F32)
    even = place_ref[CORE] == 0
    first = jnp.where(even, own, got)
    second = jnp.where(even, got, own)
    both_ref[:, :128] = jnp.where(low, first, turned(second)).astype(BF)
    both_ref[:, 128:] = jnp.where(low, turned(first), second).astype(BF)


def normed(values, gain, shift):
    center = values - jnp.mean(values, axis=-1, keepdims=True)
    spread_out = jnp.mean(center * center, axis=-1, keepdims=True)
    return center * lax.rsqrt(spread_out + EPS) * gain + shift


def gelu(value):
    return 0.5 * value * (1.0 + lax.erf(value * (2.0 ** (-0.5))))


def project_kernel(place_ref, *refs):
    (*piece_refs, mine_ref, theirs_ref, x_hbm, gain_ref, shift_ref, norm_ref, keep_ref, att_scr, x_ref, sems) = refs
    depth = len(piece_refs)
    rows, width = norm_ref.shape
    share = rows // depth
    twins = x_hbm.shape[0] // rows
    copies = []
    for z in range(depth):
        start = pl.multiple_of((z * twins + place_ref[TWIN]) * share, share)
        copies.append(pltpu.make_async_copy(x_hbm.at[pl.ds(start, share)], x_ref.at[pl.ds(z * share, share)], sems.at[z]))
        copies[-1].start()
    core = place_ref[CORE]
    block = width // depth
    for bits, piece_ref in enumerate(piece_refs):
        source = place_ref[DEEP] ^ bits
        lanes = pl.ds(pl.multiple_of(source % (depth // 2) * block, block), block)
        att_scr[source // (depth // 2), :, lanes] = piece_ref[...]
    for copy in copies:
        copy.wait()
    total = x_ref[...].astype(F32)
    for side, ref in ((core, mine_ref), (1 - core, theirs_ref)):
        total += lax.dot_general(att_scr[side], ref[...], NT, preferred_element_type=F32)
    norm_ref[...] = normed(total, gain_ref[...], shift_ref[...]).astype(BF)
    keep_ref[...] = norm_ref[pl.ds(pl.multiple_of(place_ref[DEEP] * share, share), share)]


def half_feed(arrived, ref):
    half_h = ref.shape[1] // 2
    up = jnp.dot(arrived, ref[:, :half_h], preferred_element_type=F32)
    active = gelu(up).astype(BF)
    return lax.dot_general(active, ref[:, half_h:], NT, preferred_element_type=F32)


def own_feed_kernel(norm_ref, mine_ref, arrived_ref, result_ref):
    arrived_ref[...] = rearranged(norm_ref[...], False)
    result_ref[...] = half_feed(arrived_ref[...], mine_ref)


def feed_kernel(place_ref, arrived_ref, own_ref, theirs_ref, *refs):
    *sum_refs, sum_scr = refs
    share = sum_refs[0].shape[0]
    result = own_ref[...] + half_feed(arrived_ref[...], theirs_ref)
    sum_scr[...] = rearranged(result.astype(BF), True)
    for bits, sum_ref in enumerate(sum_refs):
        sum_ref[...] = sum_scr[pl.ds(pl.multiple_of((place_ref[DEEP] ^ bits) * share, share), share)]


def final_kernel(*refs):
    *sum_refs, keep_ref, gain_ref, shift_ref, out_ref = refs
    total = keep_ref[...].astype(F32)
    for sum_ref in sum_refs:
        total += sum_ref[...].astype(F32)
    out_ref[...] = normed(total, gain_ref[...], shift_ref[...]).astype(BF)


def cache_kernel(place_ref, own_ref, got_ref, keys_ref, values_ref):
    low = low_lanes(own_ref.shape)
    own = own_ref[...].astype(F32)
    got = got_ref[got_ref.shape[0] - own.shape[0] :].astype(F32)
    even = place_ref[CORE] == 0
    first = jnp.where(even, own, got)
    second = jnp.where(even, got, own)
    keys_ref[...] = jnp.where(low, first, turned(second)).astype(BF)
    values_ref[...] = jnp.where(low, turned(first), second).astype(BF)


def exchange(value, axes):
    return lax.all_to_all(value, axes, split_axis=0, concat_axis=0, tiled=True)


def swapped(value):
    return lax.ppermute(value, "cc", [(0, 1), (1, 0)])


def crossed(values):
    size = len(values)
    return [values[0]] + [lax.ppermute(values[bits], "zz", [(i, i ^ bits) for i in range(size)]) for bits in range(1, size)]


def body(hidden_in, request_ids, w_qkv, w_out, w_up, w_down, ln1_gain, ln1_shift, ln2_gain, ln2_shift):
    copies = lax.axis_size("yh") * lax.axis_size("xx")
    cores = lax.axis_size("cc")
    depth = lax.axis_size("zz")
    twins = lax.axis_size("yl")
    rows, width = hidden_in.shape
    unit = w_qkv.shape[0]
    hidden = w_up.shape[1] // depth
    place = jnp.stack([lax.axis_index("cc"), lax.axis_index("zz"), lax.axis_index("yl")]).astype(jnp.int32)

    def call(kernel, name, out_shape, in_specs, work=0, room=8, **more):
        more["cost_estimate"] = pl.CostEstimate(flops=work, bytes_accessed=2**20, transcendentals=0)
        flat = isinstance(out_shape, tuple)
        more.setdefault("out_specs", (VM,) * len(out_shape) if flat else VM)
        params = pltpu.CompilerParams(vmem_limit_bytes=room * 2**20)
        return pl.pallas_call(kernel, out_shape=out_shape, in_specs=in_specs, compiler_params=params, name=name, **more)

    def shape(*dims):
        return jax.ShapeDtypeStruct(dims, BF)

    w_qkv, w_out, w_up, w_down, hidden_in = (pltpu.with_memory_space_constraint(x, pltpu.HBM) for x in (w_qkv, w_out, w_up, w_down, hidden_in))
    first_cols = 128 + 384
    packed = call(pack_first_kernel, "pack_first", shape(copies, cores, depth, twins, unit, first_cols), [VM, VM])(w_qkv, w_out)
    served = exchange(packed.reshape(-1, unit, first_cols), GROUP + PART).reshape(width, first_cols)
    other_hidden = swapped(hidden_in)
    other_ids = swapped(request_ids)
    held = crossed(call(pack_depth_kernel, "pack_depth", (shape(unit, 2 * hidden),) * depth, [SM, VM, VM])(place, w_up, w_down))
    held, other_hidden, other_ids = lax.optimization_barrier((held, other_hidden, other_ids))
    packed_rest = call(pack_rest_kernel, "pack_rest", shape(copies, cores, twins, depth, unit, hidden), [SM] + [VM] * depth)(place, *held)
    packed_rest, served = lax.optimization_barrier((packed_rest, served))
    rest = exchange(packed_rest.reshape(-1, depth, unit, hidden), GROUP + ("yl",)).reshape(width, hidden)

    out_part = call(take_kernel, "take", shape(width, 128), [pl.BlockSpec((width, 128), lambda i: (0, 0))], grid=(1,), out_specs=pl.BlockSpec((width, 128), lambda i: (0, 0)))(served)
    out_parts = crossed([out_part] * depth)
    id_tiles = (rows // 128, 128)
    few = rows // twins
    att_own, kv_own, send = call(
        attend_kernel,
        "attend",
        (shape(few, 128), shape(rows, 128), shape(few + rows, 128)),
        [SM, HB, HB, VM, VM, VM],
        5 * 10**9,
        16,
        scratch_shapes=[pltpu.VMEM((2, rows, width), BF)]
        + [pltpu.VMEM((2, 2 * rows, 128), BF)] * 3
        + [pltpu.VMEM((2 * rows // 128, 128), F32), pltpu.SemaphoreType.DMA((2,))],
    )(place, hidden_in, other_hidden, served, request_ids.reshape(id_tiles), other_ids.reshape(id_tiles))
    got = swapped(send)
    joined = call(join_kernel, "join", shape(few, 256), [SM, VM, VM])(place, att_own, got)
    out_parts, got = lax.optimization_barrier((out_parts, got))
    mine_out = call(assemble_kernel, "assemble", shape(width, width // cores), [SM] + [VM] * depth)(place, *out_parts)
    mine_out, joined = lax.optimization_barrier((mine_out, joined))
    pieces = crossed([joined] * depth)
    theirs_out = swapped(mine_out)
    keys_out, values_out = call(cache_kernel, "cache", (shape(rows, 128),) * 2, [SM, VM, VM], 10**9)(place, kv_own, got)

    share = few // depth
    norm, keep = call(
        project_kernel,
        "project",
        (shape(few, width), shape(share, width)),
        [SM] + [VM] * (depth + 2) + [HB, VM, VM],
        2 * 10**9,
        16,
        scratch_shapes=[pltpu.VMEM((2, few, width // 2), BF), pltpu.VMEM((few, width), BF), pltpu.SemaphoreType.DMA((depth,))],
    )(place, *pieces, mine_out, theirs_out, hidden_in, ln1_gain[None, :], ln1_shift[None, :])
    rest, norm = lax.optimization_barrier((rest, norm))
    theirs = swapped(rest)
    arrived, own_sums = call(
        own_feed_kernel,
        "own_feed",
        (shape(few, width), jax.ShapeDtypeStruct((few, width), F32)),
        [VM, VM],
        2 * 10**9,
        16,
    )(norm, rest)
    sums = call(
        feed_kernel,
        "feed",
        (shape(share, width),) * depth,
        [SM] + [VM] * 3,
        3 * 10**9,
        20,
        scratch_shapes=[pltpu.VMEM((few, width), BF)],
    )(place, arrived, own_sums, theirs)
    sums = crossed(sums)
    final = call(final_kernel, "final", shape(share, width), [VM] * (depth + 3))(*sums, keep, ln2_gain[None, :], ln2_shift[None, :])
    return (final, keys_out, values_out)


def solution(mesh):
    fine = Mesh(mesh.devices.reshape(2, 4, 2, 4, 2), GROUP + PART)
    in_specs = (
        P(GROUP, None),
        P(GROUP),
        P(GROUP + PART, None),
        P(GROUP + PART, None),
        P(GROUP + PART, None),
        P(GROUP + PART, None),
        P(),
        P(),
        P(),
        P(),
    )
    out_specs = (P(GROUP + PART, None), P(GROUP, PART), P(GROUP, PART))
    return jax.shard_map(body, mesh=fine, in_specs=in_specs, out_specs=out_specs, check_vma=False)
```

```python
import functools

import jax
import jax.numpy as jnp
from jax import lax
from jax.experimental import pallas as pl
from jax.experimental.pallas import tpu as pltpu
from jax.sharding import Mesh
from jax.sharding import PartitionSpec as P

HD = 64
BF = jnp.bfloat16
F32 = jnp.float32
EPS = 1e-05
NT = (((1,), (1,)), ((), ()))
GROUP = ("yh", "xx", "cc")
PART = ("zz", "yl")
VM = pl.BlockSpec(memory_space=pltpu.VMEM)
SM = pl.BlockSpec(memory_space=pltpu.SMEM)
HB = pl.BlockSpec(memory_space=pltpu.HBM)
CORE, DEEP, TWIN = range(3)


def low_lanes(shape):
    return lax.broadcasted_iota(jnp.int32, shape, len(shape) - 1) < HD


def turned(value):
    return pltpu.roll(value, HD, len(value.shape) - 1)


def spread():
    rows = lax.broadcasted_iota(jnp.int32, (128, 128), 0)
    cols = lax.broadcasted_iota(jnp.int32, (128, 128), 1)
    inner = cols % 64
    source = cols - inner + inner % 32 // 8 * 16 + inner // 32 * 8 + inner % 8
    return jnp.where(rows == source, 1.0, 0.0).astype(BF)


def rearranged(value, back):
    moved = spread()
    tiles = []
    for lane in range(0, value.shape[1], 128):
        tile = value[:, lane : lane + 128]
        if back:
            tiles.append(lax.dot_general(tile, moved, NT, preferred_element_type=F32).astype(BF))
        else:
            tiles.append(jnp.dot(tile, moved, preferred_element_type=F32).astype(BF))
    return jnp.concatenate(tiles, axis=1)


def replicate(row_scr, packed_hbm, sems, twin_at):
    copies = []
    for copy in range(packed_hbm.shape[0]):
        for twin in range(packed_hbm.shape[twin_at]):
            target = packed_hbm.at[copy, :, :, twin] if twin_at == 3 else packed_hbm.at[copy, :, twin]
            copies.append(pltpu.make_async_copy(row_scr, target, sems.at[copy, twin]))
            copies[-1].start()
    for copy in copies:
        copy.wait()


def pack_first_kernel(qkv_ref, out_ref, packed_ref, row_scr, sems):
    rows = qkv_ref.shape[0]
    width = qkv_ref.shape[1] // 3
    cores, depth = row_scr.shape[:2]
    low = low_lanes((rows, 128))

    def tile(kind, number):
        start = kind * width + number * 128
        return qkv_ref[:, start : start + 128]

    for core in range(cores):
        for z in range(depth):
            start = core * (width // cores) + z * 128
            parts = [out_ref[:, start : start + 128]]
            for twin in range(2):
                q_tile, k_tile = tile(0, 2 * z + twin), tile(1, 2 * z + twin)
                if core == 0:
                    parts.append(jnp.where(low, q_tile, turned(k_tile)))
                else:
                    parts.append(jnp.where(low, turned(q_tile), k_tile))
            one, two = tile(2, 2 * z), tile(2, 2 * z + 1)
            if core == 0:
                parts.append(jnp.where(low, one, turned(two)))
            else:
                parts.append(jnp.where(low, turned(one), two))
            row_scr[core, z] = jnp.concatenate(parts, axis=1).astype(BF)
    replicate(row_scr, packed_ref, sems, 3)


def pack_depth_kernel(place_ref, up_ref, down_ref, *piece_refs):
    depth = len(piece_refs)
    span = up_ref.shape[1] // depth
    for bits, piece_ref in enumerate(piece_refs):
        start = pl.multiple_of((place_ref[DEEP] ^ bits) * span, span)
        piece_ref[:, :span] = up_ref[:, pl.ds(start, span)].astype(BF)
        piece_ref[:, span:] = down_ref[:, pl.ds(start, span)].astype(BF)


def pack_rest_kernel(place_ref, *refs):
    *piece_refs, packed_ref, row_scr, sems = refs
    cores = row_scr.shape[0]
    half_h = row_scr.shape[3] // 2
    for bits, piece_ref in enumerate(piece_refs):
        z = place_ref[DEEP] ^ bits
        span = piece_ref.shape[1] // 2
        for core in range(cores):
            start = core * half_h
            row_scr[core, z] = jnp.concatenate([piece_ref[:, start : start + half_h], piece_ref[:, span + start : span + start + half_h]], axis=1)
    replicate(row_scr, packed_ref, sems, 2)


def take_kernel(served_ref, part_ref):
    part_ref[...] = served_ref[...]


def attend_kernel(place_ref, own_hbm, other_hbm, weight_ref, own_ids_ref, other_ids_ref, att_ref, kv_ref, send_ref, x_scr, q_scr, k_scr, v_scr, id_scr, sems):
    copies = [pltpu.make_async_copy(ref, x_scr.at[side], sems.at[side]) for side, ref in enumerate((own_hbm, other_hbm))]
    for copy in copies:
        copy.start()
    rows = own_hbm.shape[0]
    step = 128
    tiles = rows // step
    share = att_ref.shape[0] // tiles
    twin = place_ref[TWIN]
    weight = weight_ref[:, 128:]
    low = low_lanes((rows, 128))
    for side, ids_ref in enumerate((own_ids_ref, other_ids_ref)):
        id_scr[side * tiles : (side + 1) * tiles] = ids_ref[...].astype(F32)
        copies[side].wait()
        projected = jnp.dot(x_scr[side], weight, preferred_element_type=F32)
        projected = projected.astype(BF).astype(F32)
        vv = projected[:, 256:]
        span = slice(side * rows, (side + 1) * rows)
        v_scr[0, span] = jnp.where(low, vv, 1.0).astype(BF)
        v_scr[1, span] = jnp.where(low, 1.0, vv).astype(BF)
        cached = []
        for head in range(2):
            qk = projected[:, head * 128 : head * 128 + 128]
            keys = turned(qk)
            q_scr[head, span] = jnp.where(low, qk * (HD ** (-0.5)), 0.0).astype(BF)
            k_scr[head, span] = keys.astype(BF)
            cached.append(jnp.where(low, keys, vv if head else turned(vv)))
        both = jnp.where(twin == 0, cached[0], cached[1]).astype(BF)
        if side == 0:
            kv_ref[...] = both
        else:
            send_ref[att_ref.shape[0] :] = both
    ids_row = jnp.concatenate([id_scr[i : i + 1] for i in range(2 * tiles)], axis=1)
    low_step = low_lanes((step, 128))
    row_at = lax.broadcasted_iota(jnp.int32, (step, 128), 0)
    lane_at = lax.broadcasted_iota(jnp.int32, (step, 128), 1)
    picked = lane_at == twin * share + row_at % share
    for side in range(2):
        for pair in range(tiles // 2):
            one = side * tiles + 2 * pair
            ids_two = jnp.where(row_at < share, id_scr[one : one + 1], id_scr[one + 1 : one + 2])
            ids_col = jnp.sum(jnp.where(picked, ids_two, 0.0), axis=1, keepdims=True)
            same = ids_col == ids_row
            spans = [pl.ds(pl.multiple_of((one + i) * step + twin * share, share), share) for i in range(2)]
            mixed = []
            for head in range(2):
                queries = jnp.concatenate([q_scr[head, span] for span in spans], axis=0)
                scores = lax.dot_general(queries, k_scr[head], NT, preferred_element_type=F32)
                scores = jnp.where(same, scores, -1e30)
                peak = jnp.max(scores, axis=1, keepdims=True)
                weights = jnp.exp(scores - peak).astype(BF)
                both = jnp.dot(weights, v_scr[head], preferred_element_type=F32)
                mixed.append(both / both[:, HD - head * HD : HD - head * HD + 1])
            packed = jnp.where(low_step, mixed[0], mixed[1]).astype(BF)
            ref = send_ref if side else att_ref
            ref[pair * step : (pair + 1) * step] = packed


def join_kernel(place_ref, own_ref, got_ref, both_ref):
    rows = own_ref.shape[0]
    low = low_lanes(own_ref.shape)
    own = own_ref[...].astype(F32)
    got = got_ref[:rows].astype(F32)
    even = place_ref[CORE] == 0
    first = jnp.where(even, own, got)
    second = jnp.where(even, got, own)
    both_ref[:, :128] = jnp.where(low, first, turned(second)).astype(BF)
    both_ref[:, 128:] = jnp.where(low, turned(first), second).astype(BF)


def normed(values, gain, shift):
    center = values - jnp.mean(values, axis=-1, keepdims=True)
    spread_out = jnp.mean(center * center, axis=-1, keepdims=True)
    return center * lax.rsqrt(spread_out + EPS) * gain + shift


def gelu(value):
    return 0.5 * value * (1.0 + lax.erf(value * (2.0 ** (-0.5))))


def project_kernel(place_ref, *refs):
    (*part_refs, x_hbm, gain_ref, shift_ref, norm_ref, keep_ref, att_scr, w_scr, x_ref, sems) = refs
    depth = len(part_refs) // 3
    piece_refs = part_refs[:depth]
    rows, width = norm_ref.shape
    share = rows // depth
    twins = x_hbm.shape[0] // rows
    copies = []
    for z in range(depth):
        start = pl.multiple_of((z * twins + place_ref[TWIN]) * share, share)
        copies.append(pltpu.make_async_copy(x_hbm.at[pl.ds(start, share)], x_ref.at[pl.ds(z * share, share)], sems.at[z]))
        copies[-1].start()
    core = place_ref[CORE]
    block = width // depth
    for bits, piece_ref in enumerate(piece_refs):
        source = place_ref[DEEP] ^ bits
        lanes = pl.ds(pl.multiple_of(source % (depth // 2) * block, block), block)
        att_scr[source // (depth // 2), :, lanes] = piece_ref[...]
        lanes = pl.ds(pl.multiple_of(source * 128, 128), 128)
        w_scr[0, :, lanes] = part_refs[depth + bits][...]
        w_scr[1, :, lanes] = part_refs[2 * depth + bits][...]
    for copy in copies:
        copy.wait()
    total = x_ref[...].astype(F32)
    for index, side in enumerate((core, 1 - core)):
        total += lax.dot_general(att_scr[side], w_scr[index], NT, preferred_element_type=F32)
    norm_ref[...] = normed(total, gain_ref[...], shift_ref[...]).astype(BF)
    keep_ref[...] = norm_ref[pl.ds(pl.multiple_of(place_ref[DEEP] * share, share), share)]


def half_feed(arrived, ref):
    half_h = ref.shape[1] // 2
    up = jnp.dot(arrived, ref[:, :half_h], preferred_element_type=F32)
    active = gelu(up).astype(BF)
    return lax.dot_general(active, ref[:, half_h:], NT, preferred_element_type=F32)


def own_feed_kernel(norm_ref, mine_ref, arrived_ref, result_ref):
    arrived_ref[...] = rearranged(norm_ref[...], False)
    result_ref[...] = half_feed(arrived_ref[...], mine_ref)


def feed_kernel(targets, place_ref, arrived_ref, own_ref, theirs_ref, *sum_refs):
    share = sum_refs[0].shape[0]
    spans = [pl.ds(pl.multiple_of((place_ref[DEEP] ^ bits) * share, share), share) for bits in targets]
    arrived = jnp.concatenate([arrived_ref[span] for span in spans], axis=0)
    result = jnp.concatenate([own_ref[span] for span in spans], axis=0) + half_feed(arrived, theirs_ref)
    result = rearranged(result.astype(BF), True)
    for index, sum_ref in enumerate(sum_refs):
        sum_ref[...] = result[index * share : (index + 1) * share]


def final_kernel(*refs):
    *sum_refs, keep_ref, gain_ref, shift_ref, out_ref = refs
    total = keep_ref[...].astype(F32)
    for sum_ref in sum_refs:
        total += sum_ref[...].astype(F32)
    out_ref[...] = normed(total, gain_ref[...], shift_ref[...]).astype(BF)


def cache_kernel(place_ref, own_ref, got_ref, keys_ref, values_ref):
    low = low_lanes(own_ref.shape)
    own = own_ref[...].astype(F32)
    got = got_ref[got_ref.shape[0] - own.shape[0] :].astype(F32)
    even = place_ref[CORE] == 0
    first = jnp.where(even, own, got)
    second = jnp.where(even, got, own)
    keys_ref[...] = jnp.where(low, first, turned(second)).astype(BF)
    values_ref[...] = jnp.where(low, turned(first), second).astype(BF)


def exchange(value, axes):
    return lax.all_to_all(value, axes, split_axis=0, concat_axis=0, tiled=True)


def swapped(value):
    return lax.ppermute(value, "cc", [(0, 1), (1, 0)])


def moved(value, bits):
    return lax.ppermute(value, "zz", [(i, i ^ bits) for i in range(lax.axis_size("zz"))])


def crossed(values):
    return [values[0]] + [moved(values[bits], bits) for bits in range(1, len(values))]


def body(hidden_in, request_ids, w_qkv, w_out, w_up, w_down, ln1_gain, ln1_shift, ln2_gain, ln2_shift):
    copies = lax.axis_size("yh") * lax.axis_size("xx")
    cores = lax.axis_size("cc")
    depth = lax.axis_size("zz")
    twins = lax.axis_size("yl")
    rows, width = hidden_in.shape
    unit = w_qkv.shape[0]
    hidden = w_up.shape[1] // depth
    place = jnp.stack([lax.axis_index("cc"), lax.axis_index("zz"), lax.axis_index("yl")]).astype(jnp.int32)

    def call(kernel, name, out_shape, in_specs, work=0, room=8, **more):
        more["cost_estimate"] = pl.CostEstimate(flops=work, bytes_accessed=2**20, transcendentals=0)
        flat = isinstance(out_shape, tuple)
        more.setdefault("out_specs", (VM,) * len(out_shape) if flat else VM)
        params = pltpu.CompilerParams(vmem_limit_bytes=room * 2**20)
        return pl.pallas_call(kernel, out_shape=out_shape, in_specs=in_specs, compiler_params=params, name=name, **more)

    def shape(*dims):
        return jax.ShapeDtypeStruct(dims, BF)

    w_qkv, w_out, w_up, w_down, hidden_in = (pltpu.with_memory_space_constraint(x, pltpu.HBM) for x in (w_qkv, w_out, w_up, w_down, hidden_in))
    first_cols = 128 + 384
    sems = pltpu.SemaphoreType.DMA((copies, twins))
    packed = call(
        pack_first_kernel,
        "pack_first",
        shape(copies, cores, depth, twins, unit, first_cols),
        [VM, VM],
        out_specs=HB,
        scratch_shapes=[pltpu.VMEM((cores, depth, unit, first_cols), BF), sems],
    )(w_qkv, w_out)
    served = exchange(packed.reshape(-1, unit, first_cols), GROUP + PART).reshape(width, first_cols)
    other_hidden = swapped(hidden_in)
    other_ids = swapped(request_ids)
    held = crossed(call(pack_depth_kernel, "pack_depth", (shape(unit, 2 * hidden),) * depth, [SM, VM, VM])(place, w_up, w_down))
    held, other_hidden, other_ids = lax.optimization_barrier((held, other_hidden, other_ids))
    packed_rest = call(
        pack_rest_kernel,
        "pack_rest",
        shape(copies, cores, twins, depth, unit, hidden),
        [SM] + [VM] * depth,
        out_specs=HB,
        scratch_shapes=[pltpu.VMEM((cores, depth, unit, hidden), BF), sems],
    )(place, *held)
    packed_rest, served = lax.optimization_barrier((packed_rest, served))
    rest = exchange(packed_rest.reshape(-1, depth, unit, hidden), GROUP + ("yl",)).reshape(width, hidden)

    out_part = call(take_kernel, "take", shape(width, 128), [pl.BlockSpec((width, 128), lambda i: (0, 0))], grid=(1,), out_specs=pl.BlockSpec((width, 128), lambda i: (0, 0)))(served)
    far = moved(out_part, 3)
    out_parts = [out_part, moved(out_part, 1), None, far]
    id_tiles = (rows // 128, 128)
    few = rows // twins
    att_own, kv_own, send = call(
        attend_kernel,
        "attend",
        (shape(few, 128), shape(rows, 128), shape(few + rows, 128)),
        [SM, HB, HB, VM, VM, VM],
        5 * 10**9,
        16,
        scratch_shapes=[pltpu.VMEM((2, rows, width), BF)]
        + [pltpu.VMEM((2, 2 * rows, 128), BF)] * 3
        + [pltpu.VMEM((2 * rows // 128, 128), F32), pltpu.SemaphoreType.DMA((2,))],
    )(place, hidden_in, other_hidden, served, request_ids.reshape(id_tiles), other_ids.reshape(id_tiles))
    got = swapped(send)
    got, out_parts[1], out_parts[3] = lax.optimization_barrier((got, out_parts[1], out_parts[3]))
    out_parts[2] = moved(out_parts[3], 1)
    joined = call(join_kernel, "join", shape(few, 256), [SM, VM, VM])(place, att_own, got)
    out_parts[0], out_parts[1], out_parts[3], joined = lax.optimization_barrier((out_parts[0], out_parts[1], out_parts[3], joined))
    pieces = crossed([joined] * depth)
    out_parts[2], pieces = lax.optimization_barrier((out_parts[2], pieces))
    their_parts = [swapped(part) for part in out_parts]
    keys_out, values_out = call(cache_kernel, "cache", (shape(rows, 128),) * 2, [SM, VM, VM], 10**9)(place, kv_own, got)

    share = few // depth
    norm, keep = call(
        project_kernel,
        "project",
        (shape(few, width), shape(share, width)),
        [SM] + [VM] * (3 * depth) + [HB, VM, VM],
        2 * 10**9,
        16,
        scratch_shapes=[
            pltpu.VMEM((2, few, width // 2), BF),
            pltpu.VMEM((2, width, width // 2), BF),
            pltpu.VMEM((few, width), BF),
            pltpu.SemaphoreType.DMA((depth,)),
        ],
    )(place, *pieces, *out_parts, *their_parts, hidden_in, ln1_gain[None, :], ln1_shift[None, :])
    rest, norm = lax.optimization_barrier((rest, norm))
    norm = pltpu.with_memory_space_constraint(norm, pltpu.HBM)
    theirs = swapped(rest)
    arrived, own_sums = call(
        own_feed_kernel,
        "own_feed",
        (shape(few, width), jax.ShapeDtypeStruct((few, width), F32)),
        [VM, VM],
        2 * 10**9,
        16,
    )(norm, rest)
    sums = [None] * depth
    for targets in ((2, 3), (1, 0)):
        results = call(
            functools.partial(feed_kernel, targets),
            "feed",
            (shape(share, width),) * len(targets),
            [SM] + [VM] * 3,
            10**9,
            16,
        )(place, arrived, own_sums, theirs)
        for bits, result in zip(targets, results):
            sums[bits] = result
    sums = crossed(sums)
    final = call(final_kernel, "final", shape(share, width), [VM] * (depth + 3))(*sums, keep, ln2_gain[None, :], ln2_shift[None, :])
    return (final, keys_out, values_out)


def solution(mesh):
    fine = Mesh(mesh.devices.reshape(2, 4, 2, 4, 2), GROUP + PART)
    in_specs = (
        P(GROUP, None),
        P(GROUP),
        P(GROUP + PART, None),
        P(GROUP + PART, None),
        P(GROUP + PART, None),
        P(GROUP + PART, None),
        P(),
        P(),
        P(),
        P(),
    )
    out_specs = (P(GROUP + PART, None), P(GROUP, PART), P(GROUP, PART))
    return jax.shard_map(body, mesh=fine, in_specs=in_specs, out_specs=out_specs, check_vma=False)
```

```python
import functools

import jax
import jax.numpy as jnp
from jax import lax
from jax.experimental import pallas as pl
from jax.experimental.pallas import tpu as pltpu
from jax.sharding import Mesh
from jax.sharding import PartitionSpec as P

HD = 64
BF = jnp.bfloat16
F32 = jnp.float32
EPS = 1e-05
NT = (((1,), (1,)), ((), ()))
GROUP = ("yh", "xx", "cc")
PART = ("zz", "yl")
VM = pl.BlockSpec(memory_space=pltpu.VMEM)
SM = pl.BlockSpec(memory_space=pltpu.SMEM)
HB = pl.BlockSpec(memory_space=pltpu.HBM)
CORE, DEEP, TWIN = range(3)


def low_lanes(shape):
    return lax.broadcasted_iota(jnp.int32, shape, len(shape) - 1) < HD


def turned(value):
    return pltpu.roll(value, HD, len(value.shape) - 1)


def spread():
    rows = lax.broadcasted_iota(jnp.int32, (128, 128), 0)
    cols = lax.broadcasted_iota(jnp.int32, (128, 128), 1)
    inner = cols % 64
    source = cols - inner + inner % 32 // 8 * 16 + inner // 32 * 8 + inner % 8
    return jnp.where(rows == source, 1.0, 0.0).astype(BF)


def rearranged(value, back):
    moved = spread()
    tiles = []
    for lane in range(0, value.shape[1], 128):
        tile = value[:, lane : lane + 128]
        if back:
            tiles.append(lax.dot_general(tile, moved, NT, preferred_element_type=F32).astype(BF))
        else:
            tiles.append(jnp.dot(tile, moved, preferred_element_type=F32).astype(BF))
    return jnp.concatenate(tiles, axis=1)


def replicate(row_scr, packed_hbm, sems):
    copies = []
    for copy in range(packed_hbm.shape[0]):
        for twin in range(packed_hbm.shape[2]):
            target = packed_hbm.at[copy, :, twin]
            copies.append(pltpu.make_async_copy(row_scr, target, sems.at[copy, twin]))
            copies[-1].start()
    for copy in copies:
        copy.wait()


def pack_first_kernel(qkv_hbm, out_hbm, packed_hbm, qkv_ref, out_ref, row_scr, in_sems, sems):
    rows, width = out_ref.shape
    pairs = [(out_hbm, out_ref)]
    for kind in range(3):
        span = slice(kind * width, (kind + 1) * width)
        pairs.append((qkv_hbm.at[:, span], qkv_ref.at[:, span]))
    loads = [pltpu.make_async_copy(source, target, in_sems.at[i]) for i, (source, target) in enumerate(pairs)]
    for load in loads:
        load.start()
    cores, depth = row_scr.shape[:2]
    low = low_lanes((rows, 128))

    def tile(kind, number):
        start = kind * width + number * 128
        return qkv_ref[:, start : start + 128]

    for load in loads:
        load.wait()
    copies = []
    for core in range(cores):
        for z in range(depth):
            start = core * (width // cores) + z * 128
            parts = [out_ref[:, start : start + 128]]
            for twin in range(2):
                q_tile, k_tile = tile(0, 2 * z + twin), tile(1, 2 * z + twin)
                if core == 0:
                    parts.append(jnp.where(low, q_tile, turned(k_tile)))
                else:
                    parts.append(jnp.where(low, turned(q_tile), k_tile))
            one, two = tile(2, 2 * z), tile(2, 2 * z + 1)
            if core == 0:
                parts.append(jnp.where(low, one, turned(two)))
            else:
                parts.append(jnp.where(low, turned(one), two))
            row_scr[core, z] = jnp.concatenate(parts, axis=1).astype(BF)
        for copy in range(packed_hbm.shape[0]):
            for twin in range(packed_hbm.shape[3]):
                target = packed_hbm.at[copy, core, :, twin]
                copies.append(pltpu.make_async_copy(row_scr.at[core], target, sems.at[core, copy, twin]))
                copies[-1].start()
    for copy in copies:
        copy.wait()


def pack_depth_kernel(place_ref, up_ref, down_ref, *piece_refs):
    depth = len(piece_refs)
    span = up_ref.shape[1] // depth
    for bits, piece_ref in enumerate(piece_refs):
        start = pl.multiple_of((place_ref[DEEP] ^ bits) * span, span)
        piece_ref[:, :span] = up_ref[:, pl.ds(start, span)].astype(BF)
        piece_ref[:, span:] = down_ref[:, pl.ds(start, span)].astype(BF)


def pack_rest_kernel(place_ref, *refs):
    *piece_refs, packed_ref, row_scr, sems = refs
    cores = row_scr.shape[0]
    half_h = row_scr.shape[3] // 2
    for bits, piece_ref in enumerate(piece_refs):
        z = place_ref[DEEP] ^ bits
        span = piece_ref.shape[1] // 2
        for core in range(cores):
            start = core * half_h
            row_scr[core, z] = jnp.concatenate([piece_ref[:, start : start + half_h], piece_ref[:, span + start : span + start + half_h]], axis=1)
    replicate(row_scr, packed_ref, sems)


def take_kernel(served_ref, part_ref):
    part_ref[...] = served_ref[...]


def attend_kernel(place_ref, own_hbm, other_hbm, weight_ref, own_ids_ref, other_ids_ref, att_ref, kv_ref, send_ref, x_scr, q_scr, k_scr, v_scr, id_scr, sems):
    copies = [pltpu.make_async_copy(ref, x_scr.at[side], sems.at[side]) for side, ref in enumerate((own_hbm, other_hbm))]
    for copy in copies:
        copy.start()
    rows = own_hbm.shape[0]
    step = 128
    tiles = rows // step
    share = att_ref.shape[0] // tiles
    twin = place_ref[TWIN]
    weight = weight_ref[:, 128:]
    low = low_lanes((rows, 128))
    for side, ids_ref in enumerate((own_ids_ref, other_ids_ref)):
        id_scr[side * tiles : (side + 1) * tiles] = ids_ref[...].astype(F32)
        copies[side].wait()
        projected = jnp.dot(x_scr[side], weight, preferred_element_type=F32)
        projected = projected.astype(BF).astype(F32)
        vv = projected[:, 256:]
        span = slice(side * rows, (side + 1) * rows)
        v_scr[0, span] = jnp.where(low, vv, 1.0).astype(BF)
        v_scr[1, span] = jnp.where(low, 1.0, vv).astype(BF)
        cached = []
        for head in range(2):
            qk = projected[:, head * 128 : head * 128 + 128]
            keys = turned(qk)
            q_scr[head, span] = jnp.where(low, qk * (HD ** (-0.5)), 0.0).astype(BF)
            k_scr[head, span] = keys.astype(BF)
            cached.append(jnp.where(low, keys, vv if head else turned(vv)))
        both = jnp.where(twin == 0, cached[0], cached[1]).astype(BF)
        if side == 0:
            kv_ref[...] = both
        else:
            send_ref[att_ref.shape[0] :] = both
    ids_row = jnp.concatenate([id_scr[i : i + 1] for i in range(2 * tiles)], axis=1)
    low_step = low_lanes((step, 128))
    row_at = lax.broadcasted_iota(jnp.int32, (step, 128), 0)
    lane_at = lax.broadcasted_iota(jnp.int32, (step, 128), 1)
    picked = lane_at == twin * share + row_at % share
    for side in range(2):
        for pair in range(tiles // 2):
            one = side * tiles + 2 * pair
            ids_two = jnp.where(row_at < share, id_scr[one : one + 1], id_scr[one + 1 : one + 2])
            ids_col = jnp.sum(jnp.where(picked, ids_two, 0.0), axis=1, keepdims=True)
            same = ids_col == ids_row
            spans = [pl.ds(pl.multiple_of((one + i) * step + twin * share, share), share) for i in range(2)]
            mixed = []
            for head in range(2):
                queries = jnp.concatenate([q_scr[head, span] for span in spans], axis=0)
                scores = lax.dot_general(queries, k_scr[head], NT, preferred_element_type=F32)
                scores = jnp.where(same, scores, -1e30)
                peak = jnp.max(scores, axis=1, keepdims=True)
                weights = jnp.exp(scores - peak).astype(BF)
                both = jnp.dot(weights, v_scr[head], preferred_element_type=F32)
                mixed.append(both / both[:, HD - head * HD : HD - head * HD + 1])
            packed = jnp.where(low_step, mixed[0], mixed[1]).astype(BF)
            ref = send_ref if side else att_ref
            ref[pair * step : (pair + 1) * step] = packed


def join_kernel(place_ref, own_ref, got_ref, both_ref):
    rows = own_ref.shape[0]
    low = low_lanes(own_ref.shape)
    own = own_ref[...].astype(F32)
    got = got_ref[:rows].astype(F32)
    even = place_ref[CORE] == 0
    first = jnp.where(even, own, got)
    second = jnp.where(even, got, own)
    both_ref[:, :128] = jnp.where(low, first, turned(second)).astype(BF)
    both_ref[:, 128:] = jnp.where(low, turned(first), second).astype(BF)


def normed(values, gain, shift):
    center = values - jnp.mean(values, axis=-1, keepdims=True)
    spread_out = jnp.mean(center * center, axis=-1, keepdims=True)
    return center * lax.rsqrt(spread_out + EPS) * gain + shift


def gelu(value):
    return 0.5 * value * (1.0 + lax.erf(value * (2.0 ** (-0.5))))


def project_kernel(place_ref, *refs):
    (*part_refs, x_hbm, gain_ref, shift_ref, norm_ref, keep_ref, att_scr, w_scr, x_ref, sems) = refs
    depth = len(part_refs) // 3
    piece_refs = part_refs[:depth]
    rows, width = norm_ref.shape
    share = rows // depth
    twins = x_hbm.shape[0] // rows
    copies = []
    for z in range(depth):
        start = pl.multiple_of((z * twins + place_ref[TWIN]) * share, share)
        copies.append(pltpu.make_async_copy(x_hbm.at[pl.ds(start, share)], x_ref.at[pl.ds(z * share, share)], sems.at[z]))
        copies[-1].start()
    core = place_ref[CORE]
    block = width // depth
    for bits, piece_ref in enumerate(piece_refs):
        source = place_ref[DEEP] ^ bits
        lanes = pl.ds(pl.multiple_of(source % (depth // 2) * block, block), block)
        att_scr[source // (depth // 2), :, lanes] = piece_ref[...]
        lanes = pl.ds(pl.multiple_of(source * 128, 128), 128)
        w_scr[0, :, lanes] = part_refs[depth + bits][...]
        w_scr[1, :, lanes] = part_refs[2 * depth + bits][...]
    for copy in copies:
        copy.wait()
    total = x_ref[...].astype(F32)
    for index, side in enumerate((core, 1 - core)):
        total += lax.dot_general(att_scr[side], w_scr[index], NT, preferred_element_type=F32)
    norm_ref[...] = normed(total, gain_ref[...], shift_ref[...]).astype(BF)
    keep_ref[...] = norm_ref[pl.ds(pl.multiple_of(place_ref[DEEP] * share, share), share)]


def half_feed(arrived, ref):
    half_h = ref.shape[1] // 2
    up = jnp.dot(arrived, ref[:, :half_h], preferred_element_type=F32)
    active = gelu(up).astype(BF)
    return lax.dot_general(active, ref[:, half_h:], NT, preferred_element_type=F32)


def own_feed_kernel(norm_ref, mine_ref, arrived_ref, result_ref):
    arrived_ref[...] = rearranged(norm_ref[...], False)
    result_ref[...] = half_feed(arrived_ref[...], mine_ref)


def feed_kernel(targets, place_ref, arrived_ref, own_ref, theirs_ref, *sum_refs):
    share = sum_refs[0].shape[0]
    spans = [pl.ds(pl.multiple_of((place_ref[DEEP] ^ bits) * share, share), share) for bits in targets]
    arrived = jnp.concatenate([arrived_ref[span] for span in spans], axis=0)
    result = jnp.concatenate([own_ref[span] for span in spans], axis=0) + half_feed(arrived, theirs_ref)
    result = rearranged(result.astype(BF), True)
    for index, sum_ref in enumerate(sum_refs):
        sum_ref[...] = result[index * share : (index + 1) * share]


def final_kernel(*refs):
    *sum_refs, keep_ref, gain_ref, shift_ref, out_ref = refs
    total = keep_ref[...].astype(F32)
    for sum_ref in sum_refs:
        total += sum_ref[...].astype(F32)
    out_ref[...] = normed(total, gain_ref[...], shift_ref[...]).astype(BF)


def cache_kernel(place_ref, own_ref, got_ref, keys_ref, values_ref):
    low = low_lanes(own_ref.shape)
    own = own_ref[...].astype(F32)
    got = got_ref[got_ref.shape[0] - own.shape[0] :].astype(F32)
    even = place_ref[CORE] == 0
    first = jnp.where(even, own, got)
    second = jnp.where(even, got, own)
    keys_ref[...] = jnp.where(low, first, turned(second)).astype(BF)
    values_ref[...] = jnp.where(low, turned(first), second).astype(BF)


def exchange(value, axes):
    return lax.all_to_all(value, axes, split_axis=0, concat_axis=0, tiled=True)


def swapped(value):
    return lax.ppermute(value, "cc", [(0, 1), (1, 0)])


def moved(value, bits):
    return lax.ppermute(value, "zz", [(i, i ^ bits) for i in range(lax.axis_size("zz"))])


def crossed(values):
    return [values[0]] + [moved(values[bits], bits) for bits in range(1, len(values))]


def body(hidden_in, request_ids, w_qkv, w_out, w_up, w_down, ln1_gain, ln1_shift, ln2_gain, ln2_shift):
    copies = lax.axis_size("yh") * lax.axis_size("xx")
    cores = lax.axis_size("cc")
    depth = lax.axis_size("zz")
    twins = lax.axis_size("yl")
    rows, width = hidden_in.shape
    unit = w_qkv.shape[0]
    hidden = w_up.shape[1] // depth
    place = jnp.stack([lax.axis_index("cc"), lax.axis_index("zz"), lax.axis_index("yl")]).astype(jnp.int32)

    def call(kernel, name, out_shape, in_specs, work=0, room=8, **more):
        more["cost_estimate"] = pl.CostEstimate(flops=work, bytes_accessed=2**20, transcendentals=0)
        flat = isinstance(out_shape, tuple)
        more.setdefault("out_specs", (VM,) * len(out_shape) if flat else VM)
        params = pltpu.CompilerParams(vmem_limit_bytes=room * 2**20)
        return pl.pallas_call(kernel, out_shape=out_shape, in_specs=in_specs, compiler_params=params, name=name, **more)

    def shape(*dims):
        return jax.ShapeDtypeStruct(dims, BF)

    w_qkv, w_out, hidden_in = (pltpu.with_memory_space_constraint(x, pltpu.HBM) for x in (w_qkv, w_out, hidden_in))
    first_cols = 128 + 384
    sems = pltpu.SemaphoreType.DMA((copies, twins))
    packed = call(
        pack_first_kernel,
        "pack_first",
        shape(copies, cores, depth, twins, unit, first_cols),
        [HB, HB],
        out_specs=HB,
        scratch_shapes=[
            pltpu.VMEM((unit, 3 * width), F32),
            pltpu.VMEM((unit, width), F32),
            pltpu.VMEM((cores, depth, unit, first_cols), BF),
            pltpu.SemaphoreType.DMA((4,)),
            pltpu.SemaphoreType.DMA((cores, copies, twins)),
        ],
    )(w_qkv, w_out)
    served = exchange(packed.reshape(-1, unit, first_cols), GROUP + PART).reshape(width, first_cols)
    other_hidden = swapped(hidden_in)
    other_ids = swapped(request_ids)
    held = crossed(call(pack_depth_kernel, "pack_depth", (shape(unit, 2 * hidden),) * depth, [SM, VM, VM])(place, w_up, w_down))
    held, other_hidden, other_ids = lax.optimization_barrier((held, other_hidden, other_ids))
    packed_rest = call(
        pack_rest_kernel,
        "pack_rest",
        shape(copies, cores, twins, depth, unit, hidden),
        [SM] + [VM] * depth,
        out_specs=HB,
        scratch_shapes=[pltpu.VMEM((cores, depth, unit, hidden), BF), sems],
    )(place, *held)
    packed_rest, served = lax.optimization_barrier((packed_rest, served))
    rest = exchange(packed_rest.reshape(-1, depth, unit, hidden), GROUP + ("yl",)).reshape(width, hidden)

    out_part = call(take_kernel, "take", shape(width, 128), [pl.BlockSpec((width, 128), lambda i: (0, 0))], grid=(1,), out_specs=pl.BlockSpec((width, 128), lambda i: (0, 0)))(served)
    far = moved(out_part, 3)
    out_parts = [out_part, moved(out_part, 1), None, far]
    id_tiles = (rows // 128, 128)
    few = rows // twins
    att_own, kv_own, send = call(
        attend_kernel,
        "attend",
        (shape(few, 128), shape(rows, 128), shape(few + rows, 128)),
        [SM, HB, HB, VM, VM, VM],
        5 * 10**9,
        16,
        scratch_shapes=[pltpu.VMEM((2, rows, width), BF)]
        + [pltpu.VMEM((2, 2 * rows, 128), BF)] * 3
        + [pltpu.VMEM((2 * rows // 128, 128), F32), pltpu.SemaphoreType.DMA((2,))],
    )(place, hidden_in, other_hidden, served, request_ids.reshape(id_tiles), other_ids.reshape(id_tiles))
    got = swapped(send)
    got, out_parts[1], out_parts[3] = lax.optimization_barrier((got, out_parts[1], out_parts[3]))
    out_parts[2] = moved(out_parts[3], 1)
    joined = call(join_kernel, "join", shape(few, 256), [SM, VM, VM])(place, att_own, got)
    out_parts[0], out_parts[1], out_parts[3], joined = lax.optimization_barrier((out_parts[0], out_parts[1], out_parts[3], joined))
    pieces = crossed([joined] * depth)
    out_parts[2], pieces = lax.optimization_barrier((out_parts[2], pieces))
    their_parts = [swapped(part) for part in out_parts]
    keys_out, values_out = call(cache_kernel, "cache", (shape(rows, 128),) * 2, [SM, VM, VM], 10**9)(place, kv_own, got)

    share = few // depth
    norm, keep = call(
        project_kernel,
        "project",
        (shape(few, width), shape(share, width)),
        [SM] + [VM] * (3 * depth) + [HB, VM, VM],
        2 * 10**9,
        16,
        scratch_shapes=[
            pltpu.VMEM((2, few, width // 2), BF),
            pltpu.VMEM((2, width, width // 2), BF),
            pltpu.VMEM((few, width), BF),
            pltpu.SemaphoreType.DMA((depth,)),
        ],
    )(place, *pieces, *out_parts, *their_parts, hidden_in, ln1_gain[None, :], ln1_shift[None, :])
    rest, norm = lax.optimization_barrier((rest, norm))
    norm = pltpu.with_memory_space_constraint(norm, pltpu.HBM)
    theirs = swapped(rest)
    arrived, own_sums = call(
        own_feed_kernel,
        "own_feed",
        (shape(few, width), jax.ShapeDtypeStruct((few, width), F32)),
        [VM, VM],
        2 * 10**9,
        16,
    )(norm, rest)
    sums = [None] * depth
    for targets in ((2, 3), (1, 0)):
        results = call(
            functools.partial(feed_kernel, targets),
            "feed",
            (shape(share, width),) * len(targets),
            [SM] + [VM] * 3,
            10**9,
            16,
        )(place, arrived, own_sums, theirs)
        for bits, result in zip(targets, results):
            sums[bits] = result
    sums = crossed(sums)
    final = call(final_kernel, "final", shape(share, width), [VM] * (depth + 3))(*sums, keep, ln2_gain[None, :], ln2_shift[None, :])
    return (final, keys_out, values_out)


def solution(mesh):
    fine = Mesh(mesh.devices.reshape(2, 4, 2, 4, 2), GROUP + PART)
    in_specs = (
        P(GROUP, None),
        P(GROUP),
        P(GROUP + PART, None),
        P(GROUP + PART, None),
        P(GROUP + PART, None),
        P(GROUP + PART, None),
        P(),
        P(),
        P(),
        P(),
    )
    out_specs = (P(GROUP + PART, None), P(GROUP, PART), P(GROUP, PART))
    return jax.shard_map(body, mesh=fine, in_specs=in_specs, out_specs=out_specs, check_vma=False)
```

```python
import functools

import jax
import jax.numpy as jnp
from jax import lax
from jax.experimental import pallas as pl
from jax.experimental.pallas import tpu as pltpu
from jax.sharding import Mesh
from jax.sharding import PartitionSpec as P

HD = 64
BF = jnp.bfloat16
F32 = jnp.float32
EPS = 1e-05
NT = (((1,), (1,)), ((), ()))
GROUP = ("yh", "xx", "cc")
PART = ("zz", "yl")
VM = pl.BlockSpec(memory_space=pltpu.VMEM)
SM = pl.BlockSpec(memory_space=pltpu.SMEM)
HB = pl.BlockSpec(memory_space=pltpu.HBM)
CORE, DEEP, TWIN = range(3)


def low_lanes(shape):
    return lax.broadcasted_iota(jnp.int32, shape, len(shape) - 1) < HD


def turned(value):
    return pltpu.roll(value, HD, len(value.shape) - 1)


def spread():
    rows = lax.broadcasted_iota(jnp.int32, (128, 128), 0)
    cols = lax.broadcasted_iota(jnp.int32, (128, 128), 1)
    inner = cols % 64
    source = cols - inner + inner % 32 // 8 * 16 + inner // 32 * 8 + inner % 8
    return jnp.where(rows == source, 1.0, 0.0).astype(BF)


def rearranged(value, back):
    moved = spread()
    tiles = []
    for lane in range(0, value.shape[1], 128):
        tile = value[:, lane : lane + 128]
        if back:
            tiles.append(lax.dot_general(tile, moved, NT, preferred_element_type=F32).astype(BF))
        else:
            tiles.append(jnp.dot(tile, moved, preferred_element_type=F32).astype(BF))
    return jnp.concatenate(tiles, axis=1)


def replicate(row_scr, packed_hbm, sems):
    copies = []
    for copy in range(packed_hbm.shape[0]):
        for twin in range(packed_hbm.shape[2]):
            target = packed_hbm.at[copy, :, twin]
            copies.append(pltpu.make_async_copy(row_scr, target, sems.at[copy, twin]))
            copies[-1].start()
    for copy in copies:
        copy.wait()


def pack_first_kernel(qkv_hbm, out_hbm, packed_hbm, qkv_ref, out_ref, row_scr, in_sems, sems):
    rows, width = out_ref.shape
    pairs = [(out_hbm, out_ref)]
    for kind in range(3):
        span = slice(kind * width, (kind + 1) * width)
        pairs.append((qkv_hbm.at[:, span], qkv_ref.at[:, span]))
    loads = [pltpu.make_async_copy(source, target, in_sems.at[i]) for i, (source, target) in enumerate(pairs)]
    for load in loads:
        load.start()
    cores, depth = row_scr.shape[:2]
    low = low_lanes((rows, 128))

    def tile(kind, number):
        start = kind * width + number * 128
        return qkv_ref[:, start : start + 128]

    for load in loads:
        load.wait()
    copies = []
    for core in range(cores):
        for z in range(depth):
            start = core * (width // cores) + z * 128
            parts = [out_ref[:, start : start + 128]]
            for twin in range(2):
                q_tile, k_tile = tile(0, 2 * z + twin), tile(1, 2 * z + twin)
                if core == 0:
                    parts.append(jnp.where(low, q_tile, turned(k_tile)))
                else:
                    parts.append(jnp.where(low, turned(q_tile), k_tile))
            one, two = tile(2, 2 * z), tile(2, 2 * z + 1)
            if core == 0:
                parts.append(jnp.where(low, one, turned(two)))
            else:
                parts.append(jnp.where(low, turned(one), two))
            row_scr[core, z] = jnp.concatenate(parts, axis=1).astype(BF)
        for copy in range(packed_hbm.shape[0]):
            for twin in range(packed_hbm.shape[3]):
                target = packed_hbm.at[copy, core, :, twin]
                copies.append(pltpu.make_async_copy(row_scr.at[core], target, sems.at[core, copy, twin]))
                copies[-1].start()
    for copy in copies:
        copy.wait()


def pack_depth_kernel(place_ref, up_ref, down_ref, *piece_refs):
    depth = len(piece_refs)
    span = up_ref.shape[1] // depth
    for bits, piece_ref in enumerate(piece_refs):
        start = pl.multiple_of((place_ref[DEEP] ^ bits) * span, span)
        piece_ref[:, :span] = up_ref[:, pl.ds(start, span)].astype(BF)
        piece_ref[:, span:] = down_ref[:, pl.ds(start, span)].astype(BF)


def pack_rest_kernel(place_ref, *refs):
    *piece_refs, packed_ref, row_scr, sems = refs
    cores = row_scr.shape[0]
    half_h = row_scr.shape[3] // 2
    for bits, piece_ref in enumerate(piece_refs):
        z = place_ref[DEEP] ^ bits
        span = piece_ref.shape[1] // 2
        for core in range(cores):
            start = core * half_h
            row_scr[core, z] = jnp.concatenate([piece_ref[:, start : start + half_h], piece_ref[:, span + start : span + start + half_h]], axis=1)
    replicate(row_scr, packed_ref, sems)


def take_kernel(served_ref, part_ref):
    part_ref[...] = served_ref[...]


def attend_kernel(place_ref, own_hbm, other_hbm, weight_ref, own_ids_ref, other_ids_ref, att_ref, kv_ref, send_ref, x_scr, q_scr, k_scr, v_scr, id_scr, sems):
    copies = [pltpu.make_async_copy(ref, x_scr.at[side], sems.at[side]) for side, ref in enumerate((own_hbm, other_hbm))]
    for copy in copies:
        copy.start()
    rows = own_hbm.shape[0]
    step = 128
    tiles = rows // step
    share = att_ref.shape[0] // tiles
    twin = place_ref[TWIN]
    weight = weight_ref[:, 128:]
    low = low_lanes((rows, 128))
    for side, ids_ref in enumerate((own_ids_ref, other_ids_ref)):
        id_scr[side * tiles : (side + 1) * tiles] = ids_ref[...].astype(F32)
        copies[side].wait()
        projected = jnp.dot(x_scr[side], weight, preferred_element_type=F32)
        projected = projected.astype(BF).astype(F32)
        vv = projected[:, 256:]
        span = slice(side * rows, (side + 1) * rows)
        v_scr[0, span] = jnp.where(low, vv, 1.0).astype(BF)
        v_scr[1, span] = jnp.where(low, 1.0, vv).astype(BF)
        cached = []
        for head in range(2):
            qk = projected[:, head * 128 : head * 128 + 128]
            keys = turned(qk)
            q_scr[head, span] = jnp.where(low, qk * (HD ** (-0.5)), 0.0).astype(BF)
            k_scr[head, span] = keys.astype(BF)
            cached.append(jnp.where(low, keys, vv if head else turned(vv)))
        both = jnp.where(twin == 0, cached[0], cached[1]).astype(BF)
        if side == 0:
            kv_ref[...] = both
        else:
            send_ref[att_ref.shape[0] :] = both
    ids_row = jnp.concatenate([id_scr[i : i + 1] for i in range(2 * tiles)], axis=1)
    low_step = low_lanes((step, 128))
    row_at = lax.broadcasted_iota(jnp.int32, (step, 128), 0)
    lane_at = lax.broadcasted_iota(jnp.int32, (step, 128), 1)
    picked = lane_at == twin * share + row_at % share
    for side in range(2):
        for pair in range(tiles // 2):
            one = side * tiles + 2 * pair
            ids_two = jnp.where(row_at < share, id_scr[one : one + 1], id_scr[one + 1 : one + 2])
            ids_col = jnp.sum(jnp.where(picked, ids_two, 0.0), axis=1, keepdims=True)
            same = ids_col == ids_row
            spans = [pl.ds(pl.multiple_of((one + i) * step + twin * share, share), share) for i in range(2)]
            mixed = []
            for head in range(2):
                queries = jnp.concatenate([q_scr[head, span] for span in spans], axis=0)
                scores = lax.dot_general(queries, k_scr[head], NT, preferred_element_type=F32)
                scores = jnp.where(same, scores, -1e30)
                peak = jnp.max(scores, axis=1, keepdims=True)
                weights = jnp.exp(scores - peak).astype(BF)
                both = jnp.dot(weights, v_scr[head], preferred_element_type=F32)
                mixed.append(both / both[:, HD - head * HD : HD - head * HD + 1])
            packed = jnp.where(low_step, mixed[0], mixed[1]).astype(BF)
            ref = send_ref if side else att_ref
            ref[pair * step : (pair + 1) * step] = packed


def join_kernel(place_ref, own_ref, got_ref, both_ref):
    rows = own_ref.shape[0]
    low = low_lanes(own_ref.shape)
    own = own_ref[...].astype(F32)
    got = got_ref[:rows].astype(F32)
    even = place_ref[CORE] == 0
    first = jnp.where(even, own, got)
    second = jnp.where(even, got, own)
    both_ref[:, :128] = jnp.where(low, first, turned(second)).astype(BF)
    both_ref[:, 128:] = jnp.where(low, turned(first), second).astype(BF)


def normed(values, gain, shift):
    center = values - jnp.mean(values, axis=-1, keepdims=True)
    spread_out = jnp.mean(center * center, axis=-1, keepdims=True)
    return center * lax.rsqrt(spread_out + EPS) * gain + shift


def gelu(value):
    return 0.5 * value * (1.0 + lax.erf(value * (2.0 ** (-0.5))))


def project_kernel(place_ref, *refs):
    (*part_refs, x_hbm, gain_ref, shift_ref, norm_ref, keep_ref, att_scr, w_scr, x_ref, sems) = refs
    depth = len(part_refs) // 3
    piece_refs = part_refs[:depth]
    rows, width = norm_ref.shape
    share = rows // depth
    twins = x_hbm.shape[0] // rows
    copies = []
    for z in range(depth):
        start = pl.multiple_of((z * twins + place_ref[TWIN]) * share, share)
        copies.append(pltpu.make_async_copy(x_hbm.at[pl.ds(start, share)], x_ref.at[pl.ds(z * share, share)], sems.at[z]))
        copies[-1].start()
    core = place_ref[CORE]
    block = width // depth
    for bits, piece_ref in enumerate(piece_refs):
        source = place_ref[DEEP] ^ bits
        lanes = pl.ds(pl.multiple_of(source % (depth // 2) * block, block), block)
        att_scr[source // (depth // 2), :, lanes] = piece_ref[...]
        lanes = pl.ds(pl.multiple_of(source * 128, 128), 128)
        w_scr[0, :, lanes] = part_refs[depth + bits][...]
        w_scr[1, :, lanes] = part_refs[2 * depth + bits][...]
    for copy in copies:
        copy.wait()
    total = x_ref[...].astype(F32)
    for index, side in enumerate((core, 1 - core)):
        total += lax.dot_general(att_scr[side], w_scr[index], NT, preferred_element_type=F32)
    norm_ref[...] = normed(total, gain_ref[...], shift_ref[...]).astype(BF)
    keep_ref[...] = norm_ref[pl.ds(pl.multiple_of(place_ref[DEEP] * share, share), share)]


def half_feed(arrived, ref):
    half_h = ref.shape[1] // 2
    up = jnp.dot(arrived, ref[:, :half_h], preferred_element_type=F32)
    active = gelu(up).astype(BF)
    return lax.dot_general(active, ref[:, half_h:], NT, preferred_element_type=F32)


def own_feed_kernel(norm_ref, mine_ref, arrived_ref, result_ref):
    arrived_ref[...] = rearranged(norm_ref[...], False)
    result_ref[...] = half_feed(arrived_ref[...], mine_ref)


def feed_kernel(targets, place_ref, arrived_ref, own_ref, theirs_ref, *sum_refs):
    share = sum_refs[0].shape[0]
    spans = [pl.ds(pl.multiple_of((place_ref[DEEP] ^ bits) * share, share), share) for bits in targets]
    arrived = jnp.concatenate([arrived_ref[span] for span in spans], axis=0)
    result = jnp.concatenate([own_ref[span] for span in spans], axis=0) + half_feed(arrived, theirs_ref)
    result = rearranged(result.astype(BF), True)
    for index, sum_ref in enumerate(sum_refs):
        sum_ref[...] = result[index * share : (index + 1) * share]


def final_kernel(*refs):
    *sum_refs, keep_ref, gain_ref, shift_ref, out_ref = refs
    total = keep_ref[...].astype(F32)
    for sum_ref in sum_refs:
        total += sum_ref[...].astype(F32)
    out_ref[...] = normed(total, gain_ref[...], shift_ref[...]).astype(BF)


def cache_kernel(place_ref, own_ref, got_ref, keys_ref, values_ref):
    low = low_lanes(own_ref.shape)
    own = own_ref[...].astype(F32)
    got = got_ref[got_ref.shape[0] - own.shape[0] :].astype(F32)
    even = place_ref[CORE] == 0
    first = jnp.where(even, own, got)
    second = jnp.where(even, got, own)
    keys_ref[...] = jnp.where(low, first, turned(second)).astype(BF)
    values_ref[...] = jnp.where(low, turned(first), second).astype(BF)


def exchange(value, axes):
    return lax.all_to_all(value, axes, split_axis=0, concat_axis=0, tiled=True)


def swapped(value):
    return lax.ppermute(value, "cc", [(0, 1), (1, 0)])


def moved(value, bits):
    return lax.ppermute(value, "zz", [(i, i ^ bits) for i in range(lax.axis_size("zz"))])


def crossed(values):
    return [values[0]] + [moved(values[bits], bits) for bits in range(1, len(values))]


def body(hidden_in, request_ids, w_qkv, w_out, w_up, w_down, ln1_gain, ln1_shift, ln2_gain, ln2_shift):
    copies = lax.axis_size("yh") * lax.axis_size("xx")
    cores = lax.axis_size("cc")
    depth = lax.axis_size("zz")
    twins = lax.axis_size("yl")
    rows, width = hidden_in.shape
    unit = w_qkv.shape[0]
    hidden = w_up.shape[1] // depth
    place = jnp.stack([lax.axis_index("cc"), lax.axis_index("zz"), lax.axis_index("yl")]).astype(jnp.int32)

    def call(kernel, name, out_shape, in_specs, work=0, room=8, **more):
        more["cost_estimate"] = pl.CostEstimate(flops=work, bytes_accessed=2**20, transcendentals=0)
        flat = isinstance(out_shape, tuple)
        more.setdefault("out_specs", (VM,) * len(out_shape) if flat else VM)
        params = pltpu.CompilerParams(vmem_limit_bytes=room * 2**20)
        return pl.pallas_call(kernel, out_shape=out_shape, in_specs=in_specs, compiler_params=params, name=name, **more)

    def shape(*dims):
        return jax.ShapeDtypeStruct(dims, BF)

    plain_hidden = hidden_in
    w_qkv, w_out, hidden_in = (pltpu.with_memory_space_constraint(x, pltpu.HBM) for x in (w_qkv, w_out, hidden_in))
    first_cols = 128 + 384
    sems = pltpu.SemaphoreType.DMA((copies, twins))
    packed = call(
        pack_first_kernel,
        "pack_first",
        shape(copies, cores, depth, twins, unit, first_cols),
        [HB, HB],
        out_specs=HB,
        scratch_shapes=[
            pltpu.VMEM((unit, 3 * width), F32),
            pltpu.VMEM((unit, width), F32),
            pltpu.VMEM((cores, depth, unit, first_cols), BF),
            pltpu.SemaphoreType.DMA((4,)),
            pltpu.SemaphoreType.DMA((cores, copies, twins)),
        ],
    )(w_qkv, w_out)
    served = exchange(packed.reshape(-1, unit, first_cols), GROUP + PART).reshape(width, first_cols)
    other_hidden = swapped(hidden_in)
    other_ids = swapped(request_ids)
    held = crossed(call(pack_depth_kernel, "pack_depth", (shape(unit, 2 * hidden),) * depth, [SM, VM, VM])(place, w_up, w_down))
    held, other_hidden, other_ids = lax.optimization_barrier((held, other_hidden, other_ids))
    packed_rest = call(
        pack_rest_kernel,
        "pack_rest",
        shape(copies, cores, twins, depth, unit, hidden),
        [SM] + [VM] * depth,
        out_specs=HB,
        scratch_shapes=[pltpu.VMEM((cores, depth, unit, hidden), BF), sems],
    )(place, *held)
    packed_rest, served = lax.optimization_barrier((packed_rest, served))
    rest = exchange(packed_rest.reshape(-1, depth, unit, hidden), GROUP + ("yl",)).reshape(width, hidden)

    out_part = call(take_kernel, "take", shape(width, 128), [pl.BlockSpec((width, 128), lambda i: (0, 0))], grid=(1,), out_specs=pl.BlockSpec((width, 128), lambda i: (0, 0)))(served)
    far = moved(out_part, 3)
    out_parts = [out_part, moved(out_part, 1), None, far]
    id_tiles = (rows // 128, 128)
    few = rows // twins
    att_own, kv_own, send = call(
        attend_kernel,
        "attend",
        (shape(few, 128), shape(rows, 128), shape(few + rows, 128)),
        [SM, HB, HB, VM, VM, VM],
        5 * 10**9,
        16,
        scratch_shapes=[pltpu.VMEM((2, rows, width), BF)]
        + [pltpu.VMEM((2, 2 * rows, 128), BF)] * 3
        + [pltpu.VMEM((2 * rows // 128, 128), F32), pltpu.SemaphoreType.DMA((2,))],
    )(place, hidden_in, other_hidden, served, request_ids.reshape(id_tiles), other_ids.reshape(id_tiles))
    got = swapped(send)
    got, out_parts[1], out_parts[3] = lax.optimization_barrier((got, out_parts[1], out_parts[3]))
    out_parts[2] = moved(out_parts[3], 1)
    joined = call(join_kernel, "join", shape(few, 256), [SM, VM, VM])(place, att_own, got)
    out_parts[0], out_parts[1], out_parts[3], joined = lax.optimization_barrier((out_parts[0], out_parts[1], out_parts[3], joined))
    pieces = crossed([joined] * depth)
    out_parts[2], pieces = lax.optimization_barrier((out_parts[2], pieces))
    their_parts = [swapped(part) for part in out_parts]
    keys_out, values_out = call(cache_kernel, "cache", (shape(rows, 128),) * 2, [SM, VM, VM], 10**9)(place, kv_own, got)

    share = few // depth
    norm, keep = call(
        project_kernel,
        "project",
        (shape(few, width), shape(share, width)),
        [SM] + [VM] * (3 * depth) + [HB, VM, VM],
        2 * 10**9,
        16,
        scratch_shapes=[
            pltpu.VMEM((2, few, width // 2), BF),
            pltpu.VMEM((2, width, width // 2), BF),
            pltpu.VMEM((few, width), BF),
            pltpu.SemaphoreType.DMA((depth,)),
        ],
    )(place, *pieces, *out_parts, *their_parts, plain_hidden, ln1_gain[None, :], ln1_shift[None, :])
    rest, norm = lax.optimization_barrier((rest, norm))
    norm = pltpu.with_memory_space_constraint(norm, pltpu.HBM)
    theirs = swapped(rest)
    arrived, own_sums = call(
        own_feed_kernel,
        "own_feed",
        (shape(few, width), jax.ShapeDtypeStruct((few, width), F32)),
        [VM, VM],
        2 * 10**9,
        16,
    )(norm, rest)
    sums = [None] * depth
    for targets in ((2, 3), (1, 0)):
        results = call(
            functools.partial(feed_kernel, targets),
            "feed",
            (shape(share, width),) * len(targets),
            [SM] + [VM] * 3,
            10**9,
            16,
        )(place, arrived, own_sums, theirs)
        for bits, result in zip(targets, results):
            sums[bits] = result
    sums = crossed(sums)
    final = call(final_kernel, "final", shape(share, width), [VM] * (depth + 3))(*sums, keep, ln2_gain[None, :], ln2_shift[None, :])
    return (final, keys_out, values_out)


def solution(mesh):
    fine = Mesh(mesh.devices.reshape(2, 4, 2, 4, 2), GROUP + PART)
    in_specs = (
        P(GROUP, None),
        P(GROUP),
        P(GROUP + PART, None),
        P(GROUP + PART, None),
        P(GROUP + PART, None),
        P(GROUP + PART, None),
        P(),
        P(),
        P(),
        P(),
    )
    out_specs = (P(GROUP + PART, None), P(GROUP, PART), P(GROUP, PART))
    return jax.shard_map(body, mesh=fine, in_specs=in_specs, out_specs=out_specs, check_vma=False)
```
